256 devices in a mesh: section: 2 (over core), row: 8 (over x_hi, y), col: 16 (over z, x_lo).
Axes of the slice: x: 4 (x_hi: 2, x_lo: 2; x = x_hi * 2 + x_lo), y: 4, z: 8, core: 2. Of those that a mesh axis runs over, the one named last changes fastest.
Arguments:
- section_input: bfloat16 [128, 245760], P('row', ('section', 'col')), may hold values from -6 to 6
- cache_three: bfloat16 [128, 122880], P('row', ('section', 'col')), may hold values from -6 to 6
- gain_three: float32 [192], replicated, may hold values from 0.25 to 1.75
- bias_three: float32 [192], replicated, may hold values from -2 to 2
- weight_three: bfloat16 [27, 36864], replicated, may hold values from -0.078125 to 0.078125
- weight_up: bfloat16 [9, 18432], replicated, may hold values from -0.15625 to 0.15625
- bias_up: float32 [96], replicated, may hold values from -2 to 2
- cache_four: bfloat16 [256, 122880], P('row', ('section', 'col')), may hold values from -6 to 6
- gain_four: float32 [96], replicated, may hold values from 0.25 to 1.75
- weight_four: bfloat16 [27, 9216], replicated, may hold values from -0.125 to 0.125
- bias_four: float32 [96], replicated, may hold values from -2 to 2
Outputs:
- frame_out: bfloat16 [256, 245760], P('row', ('section', 'col'))
The draws below stay inside these ranges and needn't reach their ends.
All inputs are finite; a program needn't handle non-finite values.
Results may differ from the reference program's by a relative error of at most 0.0085.
Values may be sent and summed in bfloat16 or wider, within the bound.
A program may use at most 64 MiB of HBM per device.

```python
import jax
import jax.numpy as jnp
from jax import lax

C3 = 192
C4 = 96
FRAMES = 4
H3 = 128
W3 = 320
H4 = 256
W4 = 640


def steps_of(stream_key, dims, split, least, high):
    level = 1.0
    for position, shards_of in split:
        steps = jax.random.uniform(jax.random.fold_in(jax.random.fold_in(stream_key, 6), position), (shards_of,), jnp.float32, least / len(split), high / len(split))
        level = level * jnp.repeat(jnp.exp(steps), dims[position] // shards_of).reshape((-1,) + (1,) * (len(dims) - 1 - position))
    return level


def centred(key, extent, spread, reach, pieces=(), held_as=jnp.bfloat16):
    drawn = spread * jax.random.normal(key, extent, jnp.float32)
    if pieces:
        drawn = drawn * steps_of(key, extent, pieces, -0.22, 0.18)
    return jnp.clip(drawn, -reach, reach).astype(held_as)


def setup_inputs(seed: int = 0) -> dict:
    splits = jax.random.split(jax.random.key(seed), 12)
    section_input = centred(splits[0], (H3, W3 * FRAMES * C3), 1.0, 6.0, ((0, 8), (1, 32)))
    cache_three = centred(splits[1], (H3, W3 * 2 * C3), 1.0, 6.0, ((0, 8), (1, 32)))
    gain_three = jnp.clip(1.0 + 0.15 * jax.random.normal(splits[2], (C3,), jnp.float32), 0.25, 1.75)
    bias_three = centred(splits[3], (C3,), 0.3, 2.0, (), jnp.float32)
    weight_three = centred(splits[4], (27, C3 * C3), (27 * C3) ** -0.5, 0.078125)
    weight_up = centred(splits[5], (9, C4 * C3), (9 * C3) ** -0.5, 0.15625)
    bias_up = centred(splits[6], (C4,), 0.3, 2.0, (), jnp.float32)
    cache_four = centred(splits[7], (H4, W4 * 2 * C4), 1.0, 6.0, ((0, 8), (1, 32)))
    gain_four = jnp.clip(1.0 + 0.15 * jax.random.normal(splits[8], (C4,), jnp.float32), 0.25, 1.75)
    weight_four = centred(splits[9], (27, C4 * C4), (27 * C4) ** -0.5, 0.125)
    bias_four = centred(splits[10], (C4,), 0.3, 2.0, (), jnp.float32)
    return {"section_input": section_input, "cache_three": cache_three, "gain_three": gain_three, "bias_three": bias_three, "weight_three": weight_three, "weight_up": weight_up, "bias_up": bias_up, "cache_four": cache_four, "gain_four": gain_four, "weight_four": weight_four, "bias_four": bias_four}


EPSILON = 1e-06

def norm_act(values, gain):
    widened = values.astype(jnp.float32)
    meansq = lax.optimization_barrier(jnp.mean(widened * widened, axis=-1, keepdims=True))
    scaled = widened * lax.rsqrt(meansq + EPSILON) * gain
    return jax.nn.silu(scaled).astype(jnp.bfloat16)

def causal_kernel(flat_weight, in_ch):
    out_ch = flat_weight.shape[1] // in_ch
    shaped = flat_weight.reshape(3, 3, 3, out_ch, in_ch).transpose(1, 2, 0, 4, 3)
    return shaped.reshape(3, 3, 3 * in_ch, out_ch)

def spatial_kernel(flat_weight, in_ch):
    out_ch = flat_weight.shape[1] // in_ch
    return flat_weight.reshape(3, 3, out_ch, in_ch).transpose(0, 1, 3, 2)

def run_conv(batch, kernel):
    return lax.conv_general_dilated(batch, kernel, (1, 1), 'VALID', dimension_numbers=('NHWC', 'HWIO', 'NHWC'), preferred_element_type=jnp.float32)

def causal_frames(stacked, kernel, in_ch, count):
    padded = jnp.pad(stacked, ((1, 1), (1, 1), (0, 0)))
    outputs = []
    for frame_pos in range(count):
        window = padded[:, :, frame_pos * in_ch:(frame_pos + 3) * in_ch]
        outputs.append(run_conv(window[None], kernel)[0])
    return jnp.stack(outputs)

def reference(section_input, cache_three, gain_three, bias_three, weight_three, weight_up, bias_up, cache_four, gain_four, weight_four, bias_four):
    features = section_input.reshape(H3, W3, FRAMES, C3)
    active_three = norm_act(features, gain_three).reshape(H3, W3, FRAMES * C3)
    stacked = jnp.concatenate([cache_three.reshape(H3, W3, 2 * C3), active_three], axis=2)
    conv_three = causal_frames(stacked, causal_kernel(weight_three, C3), C3, FRAMES) + bias_three
    result_three = (features.transpose(2, 0, 1, 3).astype(jnp.float32) + conv_three).astype(jnp.bfloat16)
    up_kernel = spatial_kernel(weight_up, C3)
    four_inputs = []
    for frame_pos in range(FRAMES):
        upsampled = jnp.repeat(jnp.repeat(result_three[frame_pos], 2, axis=0), 2, axis=1)
        padded = jnp.pad(upsampled, ((1, 1), (1, 1), (0, 0)))
        four_inputs.append((run_conv(padded[None], up_kernel)[0] + bias_up).astype(jnp.bfloat16))
    section_four_in = jnp.stack(four_inputs)
    active_four = norm_act(section_four_in, gain_four).transpose(1, 2, 0, 3).reshape(H4, W4, FRAMES * C4)
    stacked_four = jnp.concatenate([cache_four.reshape(H4, W4, 2 * C4), active_four], axis=2)
    conv_four = causal_frames(stacked_four, causal_kernel(weight_four, C4), C4, FRAMES) + bias_four
    result = (section_four_in.astype(jnp.float32) + conv_four).astype(jnp.bfloat16)
    return result.transpose(1, 2, 0, 3).reshape(H4, W4 * FRAMES * C4)
```

```python
import functools

import jax
import jax.numpy as jnp
from jax import lax
from jax.experimental import pallas as pl
from jax.experimental.pallas import tpu as pltpu
from jax.sharding import PartitionSpec as P

EPSILON = 1e-06
MESH = pl.DeviceIdType.MESH
BF = jnp.bfloat16
F32 = jnp.float32
C3 = 192
C4 = 96
ROWS = 16
COLS = 10
FRAMES = 4
BLOCK = 24
X_LANES = COLS * FRAMES * C3
P_LANES = COLS * 2 * C3
Q_LANES = 2 * COLS * 2 * C4
EDGE = X_LANES + P_LANES + Q_LANES
CORNER = 1536 + 768 + 256


def widen(value, lanes):
    pad = lanes - value.shape[1]
    return jnp.concatenate([value, jnp.zeros((value.shape[0], pad), value.dtype)], axis=1)


def norm_act(values, gain, channels):
    meansq = jnp.sum(values * values, axis=-1, keepdims=True) * (1.0 / channels)
    scaled = values * lax.rsqrt(meansq + EPSILON) * gain
    return scaled / (1.0 + jnp.exp(-scaled))


def rounded(values):
    return values.astype(BF).astype(F32)


def by_tap(chunk, outs, stride, take):
    taps = chunk.shape[0]
    full = -(-taps // 8) * 8
    wide = jnp.concatenate([chunk, jnp.zeros((full - taps, chunk.shape[1]), chunk.dtype)], 0).astype(F32)
    pieces = []
    for start, count in take:
        stacked = jnp.stack(
            [widen(wide[:, o * stride + start : o * stride + start + count], 128) if count < 128 else
             wide[:, o * stride + start : o * stride + start + count] for o in range(outs)], 0)
        pieces.append(jnp.swapaxes(stacked, 0, 1))
    return pieces


def kernel(
    sizes,
    x_hbm, p_hbm, q_hbm, w3_hbm, wu_hbm, w4_hbm, g3, b3, bu, g4, b4,
    out,
    xv, pv, qv, w3v, wuv, w4v,
    top, bottom, corner_send,
    from_up, from_down, corner_recv, xl, xr, pl_, pr, ql, qr,
    xs, ps, act, act_one, wt3, wtu, wt4, r3s, s4, a4, resid, qext, outs,
    load_sem, send_sem, recv_sem,
):
    row_count, section_count, col_count = sizes
    r = lax.axis_index("row")
    flat_count = section_count * col_count
    g = lax.axis_index("section") * col_count + lax.axis_index("col")
    up, down = lax.rem(r + row_count - 1, row_count), lax.rem(r + 1, row_count)
    left, right = lax.rem(g + flat_count - 1, flat_count), lax.rem(g + 1, flat_count)

    def device(row, flat):
        return {"row": row, "section": flat // col_count, "col": lax.rem(flat, col_count)}

    neighbours = [(up, left), (up, g), (up, right), (r, left), (r, right), (down, left), (down, g), (down, right)]

    loads = [
        pltpu.make_async_copy(src, dst, load_sem.at[i])
        for i, (src, dst) in enumerate(
            ((x_hbm, xv), (p_hbm, pv), (q_hbm, qv), (wu_hbm, wuv), (w4_hbm, w4v), (w3_hbm, w3v))
        )
    ]
    for load in loads:
        load.start()

    barrier = pltpu.get_barrier_semaphore()
    for row, flat in neighbours:
        pl.semaphore_signal(barrier, inc=1, device_id=device(row, flat), device_id_type=MESH)

    for load in loads[:3]:
        load.wait()
    for buf, rows3, rows4 in ((top, (0, 2), (0, 2)), (bottom, (ROWS - 2, ROWS), (2 * ROWS - 2, 2 * ROWS))):
        buf[:, 0:X_LANES] = xv[rows3[0] : rows3[1], :]
        buf[:, X_LANES : X_LANES + P_LANES] = pv[rows3[0] : rows3[1], :]
        buf[:, X_LANES + P_LANES : EDGE] = qv[rows4[0] : rows4[1], :]
    for index, (rows3, rows4, high) in enumerate(
        (
            ((0, 2), (0, 2), False),
            ((0, 2), (0, 2), True),
            ((ROWS - 2, ROWS), (2 * ROWS - 2, 2 * ROWS), False),
            ((ROWS - 2, ROWS), (2 * ROWS - 2, 2 * ROWS), True),
        )
    ):
        xo, po, qo = (X_LANES - 1536, P_LANES - 768, Q_LANES - 256) if high else (0, 0, 0)
        corner_send[index, :, 0:1536] = xv[rows3[0] : rows3[1], xo : xo + 1536]
        corner_send[index, :, 1536:2304] = pv[rows3[0] : rows3[1], po : po + 768]
        corner_send[index, :, 2304:2560] = qv[rows4[0] : rows4[1], qo : qo + 256]

    pl.semaphore_wait(barrier, len(neighbours))

    plan = [
        (top, from_down, up, g),
        (bottom, from_up, down, g),
        (corner_send.at[0], corner_recv.at[3], up, left),
        (corner_send.at[1], corner_recv.at[2], up, right),
        (corner_send.at[2], corner_recv.at[1], down, left),
        (corner_send.at[3], corner_recv.at[0], down, right),
        (xv.at[:, 0:1536], xr, r, left),
        (xv.at[:, X_LANES - 1536 : X_LANES], xl, r, right),
        (pv.at[:, 0:768], pr, r, left),
        (pv.at[:, P_LANES - 768 : P_LANES], pl_, r, right),
        (qv.at[:, 0:256], qr, r, left),
        (qv.at[:, Q_LANES - 256 : Q_LANES], ql, r, right),
    ]
    copies = [
        pltpu.make_async_remote_copy(
            src_ref=src,
            dst_ref=dst,
            send_sem=send_sem.at[i],
            recv_sem=recv_sem.at[i],
            device_id=device(row, flat),
            device_id_type=MESH,
        )
        for i, (src, dst, row, flat) in enumerate(plan)
    ]
    for copy in copies:
        copy.start()

    wt3[...] = jnp.zeros_like(wt3)
    wtu[...] = jnp.zeros_like(wtu)
    wt4[...] = jnp.zeros_like(wt4)
    xs[...] = jnp.zeros_like(xs)
    ps[...] = jnp.zeros_like(ps)
    a4[...] = jnp.zeros_like(a4)
    r3s[0:96, :] = jnp.zeros((96, 768), BF)
    r3s[13 * 96 : 14 * 96, :] = jnp.zeros((96, 768), BF)

    loads[3].wait()

    def up_weights(group, _):
        chunk = wuv[:, pl.ds(pl.multiple_of(group * 16 * C3, 128), 16 * C3)]
        pieces = by_tap(chunk, 16, C3, ((0, 128), (128, 64)))
        for half, taps in enumerate(pieces):
            tap = [[taps[3 * dy + dx] for dx in range(3)] for dy in range(3)]
            across = [
                {(0, 0): line[0], (0, 1): line[1] + line[2], (1, 1): line[0] + line[1], (1, 2): line[2]} for line in tap
            ]
            for (px, dx), _first in across[0].items():
                vals = [line[(px, dx)] for line in across]
                for py, slots in enumerate(((vals[0], vals[1] + vals[2]), (vals[0] + vals[1], vals[2]))):
                    for slot, val in enumerate(slots):
                        lane = dx * 512 + slot * 256 + half * 128
                        wtu[py, pl.ds(pl.multiple_of(px * 128 + group * 16, 16), 16), lane : lane + 128] = val.astype(BF)
        return 0

    lax.fori_loop(0, 6, up_weights, 0)

    loads[4].wait()

    def four_weights(group, _):
        chunk = w4v[:, pl.ds(pl.multiple_of(group * 16 * C4, 128), 16 * C4)]
        (taps,) = by_tap(chunk, 16, C4, ((0, C4),))
        for t in range(3):
            for dx in range(3):
                for dy in range(3):
                    val = taps[9 * t + 3 * dy + dx].astype(BF)
                    for py in range(2):
                        lane = (t * 3 + dx) * 512 + (dy + py) * 128
                        wt4[pl.ds(pl.multiple_of(py * 128 + group * 16, 16), 16), lane : lane + 128] = val
        return 0

    lax.fori_loop(0, 6, four_weights, 0)

    loads[5].wait()

    def three_weights(group, _):
        chunk = w3v[:, pl.ds(pl.multiple_of(group * 16 * C3, 128), 16 * C3)]
        pieces = by_tap(chunk, 16, C3, ((0, 128), (128, 64)))
        for half, taps in enumerate(pieces):
            for t in range(3):
                for dx in range(3):
                    for dy in range(3):
                        lane = ((t * 3 + dx) * 3 + dy) * 256 + half * 128
                        wt3[pl.ds(pl.multiple_of(group * 16, 16), 16), lane : lane + 128] = taps[
                            9 * t + 3 * dy + dx
                        ].astype(BF)
        return 0

    lax.fori_loop(0, 12, three_weights, 0)

    for copy in copies:
        copy.wait()

    at_top, at_bottom, at_left, at_right = r == 0, r == row_count - 1, g == 0, g == flat_count - 1

    def keep(value, outside):
        return jnp.where(outside, jnp.zeros_like(value), value)

    for je in range(14):
        j = je - 2
        for frames, buf, main, low, high, edge_base, corner_base in (
            (FRAMES, xs, xv, xl, xr, 0, 0),
            (2, ps, pv, pl_, pr, X_LANES, 1536),
        ):
            wide = frames * C3
            if j < 0:
                side = at_left
                mid = keep(low[:, je * wide : (je + 1) * wide].astype(F32), side)
                above = corner_recv[0, :, corner_base + je * wide : corner_base + (je + 1) * wide].astype(F32)
                below = corner_recv[2, :, corner_base + je * wide : corner_base + (je + 1) * wide].astype(F32)
            elif j >= COLS:
                side = at_right
                jr = j - COLS
                mid = keep(high[:, jr * wide : (jr + 1) * wide].astype(F32), side)
                above = corner_recv[1, :, corner_base + jr * wide : corner_base + (jr + 1) * wide].astype(F32)
                below = corner_recv[3, :, corner_base + jr * wide : corner_base + (jr + 1) * wide].astype(F32)
            else:
                side = jnp.bool_(False)
                mid = main[:, j * wide : (j + 1) * wide].astype(F32)
                above = from_up[:, edge_base + j * wide : edge_base + (j + 1) * wide].astype(F32)
                below = from_down[:, edge_base + j * wide : edge_base + (j + 1) * wide].astype(F32)
            above = keep(above, jnp.logical_or(side, at_top))
            below = keep(below, jnp.logical_or(side, at_bottom))
            for k in range(frames):
                base = (je * frames + k) * BLOCK
                lanes = slice(k * C3, (k + 1) * C3)
                buf[base : base + 16, 0:C3] = mid[:, lanes]
                buf[base + 16 : base + 18, 0:C3] = below[:, lanes]
                buf[base + 22 : base + 24, 0:C3] = above[:, lanes]

    gain3 = widen(g3[...].reshape(1, C3), 256)
    bias3 = widen(b3[...].reshape(1, C3), 256)

    def build(je, _):
        raw = xs[pl.ds(pl.multiple_of(je * 96, 32), 96), :]
        new = norm_act(raw, gain3, C3).reshape(4, BLOCK, 256)
        old = ps[pl.ds(pl.multiple_of(je * 48, 16), 48), :].reshape(2, BLOCK, 256)
        frames = jnp.concatenate([old, new], 0)
        for slot, shift in enumerate((1, 0, BLOCK - 1)):
            moved = pltpu.roll(frames, shift, axis=1) if shift else frames
            lanes = slice(slot * 256, (slot + 1) * 256)
            act[pl.ds(pl.multiple_of(je * 144, 16), 144), lanes] = moved.reshape(144, 256).astype(BF)
            act_one[pl.ds(pl.multiple_of(je * 96, 32), 96), lanes] = moved[1:5].reshape(96, 256).astype(BF)
        return 0

    lax.fori_loop(0, 14, build, 0)

    def three(chunk, _):
        parts = []
        for t in range(3):
            for dx in range(3):
                rows = []
                for j in range(4):
                    je = chunk * 4 + j + dx
                    if t == 1:
                        rows.append(act_one[pl.ds(pl.multiple_of(je * 96, 32), 96), :])
                    else:
                        rows.append(act[pl.ds(pl.multiple_of(je * 144 + 24 * t, 16), 96), :])
                parts.append(jnp.concatenate(rows, 0))
        total = lax.dot_general(
            jnp.concatenate(parts, 1), wt3[...], (((1,), (1,)), ((), ())), preferred_element_type=F32
        )
        total = xs[pl.ds(pl.multiple_of(chunk * 384 + 96, 32), 384), :] + (total + bias3)
        total = total.reshape(16, BLOCK, 256)
        blk = lax.broadcasted_iota(jnp.int32, (16, BLOCK, 256), 0) + chunk * 16
        rr = lax.broadcasted_iota(jnp.int32, (16, BLOCK, 256), 1)
        lowest = jnp.where(at_left, 4, 0)
        highest = jnp.where(at_right, 44, 48)
        up_row = jnp.where(at_top, 23, -1)
        down_row = jnp.where(at_bottom, 16, -1)
        inside = (blk >= lowest) & (blk < highest) & (rr != up_row) & (rr != down_row)
        total = rounded(jnp.where(inside, total, 0.0))
        for slot, shift in enumerate((1, 0, BLOCK - 1)):
            moved = pltpu.roll(total, shift, axis=1) if shift else total
            r3s[pl.ds(pl.multiple_of(chunk * 384 + 96, 32), 384), slot * 256 : (slot + 1) * 256] = moved.reshape(
                384, 256
            ).astype(BF)
        return 0

    lax.fori_loop(0, 3, three, 0)

    bias_u = bu[...].reshape(1, C4)
    bias_u = jnp.concatenate([widen(bias_u, 128)] * 2, 1)

    def upsample(chunk, _):
        for py in range(2):
            parts = [
                r3s[pl.ds(pl.multiple_of(chunk * 384 + dx * 96, 32), 384), py * 256 : py * 256 + 512]
                for dx in range(3)
            ]
            total = lax.dot_general(
                jnp.concatenate(parts, 1), wtu[py], (((1,), (1,)), ((), ())), preferred_element_type=F32
            )
            s4[py, pl.ds(pl.multiple_of(chunk * 384, 128), 384), :] = total + bias_u
        return 0

    lax.fori_loop(0, 3, upsample, 0)

    gain4 = widen(g4[...].reshape(1, C4), 128)

    def four_in(jj, _):
        for px in range(2):
            acts = []
            at = jj * 2 + px
            for py in range(2):
                value = rounded(s4[py, pl.ds(pl.multiple_of(jj * 96, 32), 96), px * 128 : px * 128 + 128])
                shaped = value.reshape(4, BLOCK, 128)
                resid[pl.ds(pl.multiple_of(at * 64, 64), 64), py * 128 : py * 128 + 128] = shaped[:, 0:16].reshape(64, 128)
                active = norm_act(value, gain4, C4).reshape(4, BLOCK, 128)
                rr = lax.broadcasted_iota(jnp.int32, (4, BLOCK, 128), 1)
                line = jnp.where(at_bottom, 16, -1) if py == 0 else jnp.where(at_top, 23, -1)
                column = jnp.logical_or(jnp.logical_and(at_left, at < 2), jnp.logical_and(at_right, at > 21))
                line = jnp.where(column, -2, line)
                active = jnp.where(jnp.logical_or(rr == line, line == -2), 0.0, active)
                acts.append(active)
            slots = (
                pltpu.roll(acts[1], 1, axis=1),
                acts[0],
                acts[1],
                pltpu.roll(acts[0], BLOCK - 1, axis=1),
            )
            for slot, value in enumerate(slots):
                a4[pl.ds(pl.multiple_of(at * 96 + 32, 32), 64), slot * 128 : slot * 128 + 128] = (
                    value[:, 0:16].reshape(64, 128).astype(BF)
                )
        return 0

    lax.fori_loop(0, 12, four_in, 0)

    qext[...] = jnp.zeros_like(qext)
    edge_q = X_LANES + P_LANES
    qext[0:32, 256 : 256 + Q_LANES] = qv[...]
    qext[0:32, 0:256] = keep(ql[...], at_left)
    qext[0:32, 256 + Q_LANES : 512 + Q_LANES] = keep(qr[...], at_right)
    for base, edge, outside, low_corner, high_corner in (
        (32, from_up, at_top, 0, 1),
        (40, from_down, at_bottom, 2, 3),
    ):
        qext[base : base + 2, 256 : 256 + Q_LANES] = keep(edge[:, edge_q:EDGE], outside)
        qext[base : base + 2, 0:256] = keep(corner_recv[low_corner, :, 2304:2560], jnp.logical_or(outside, at_left))
        qext[base : base + 2, 256 + Q_LANES : 512 + Q_LANES] = keep(
            corner_recv[high_corner, :, 2304:2560], jnp.logical_or(outside, at_right)
        )
    want = lax.broadcasted_iota(jnp.int32, (64, 48), 0)
    have = lax.broadcasted_iota(jnp.int32, (64, 48), 1)
    slot = want >> 4
    i = want & 15
    source = jnp.where(
        slot == 0,
        jnp.where(i == 0, 33, 2 * i - 1),
        jnp.where(slot == 1, 2 * i, jnp.where(slot == 2, 2 * i + 1, jnp.where(i == 15, 40, 2 * i + 2))),
    )
    pick = jnp.where(source == have, 1.0, 0.0).astype(BF)
    for xe in range(22):
        start = 64 + xe * 192
        low = start // 128 * 128
        picked = jnp.dot(pick, qext[:, low : low + 256], preferred_element_type=F32)
        for t in range(2):
            off = start - low + t * C4
            piece = picked[:, off : off + C4].astype(BF)
            for s in range(4):
                a4[(xe + 1) * 96 + t * 16 : (xe + 1) * 96 + t * 16 + 16, s * 128 : s * 128 + C4] = piece[
                    s * 16 : s * 16 + 16
                ]

    bias4 = widen(b4[...].reshape(1, C4), 128)
    bias4 = jnp.concatenate([bias4, bias4], 1)

    def four(chunk, _):
        parts = []
        for t in range(3):
            for dx in range(3):
                parts.append(
                    jnp.concatenate(
                        [
                            a4[pl.ds(pl.multiple_of((chunk * 5 + x + 1 + dx) * 96 + t * 16, 16), 64), :]
                            for x in range(5)
                        ],
                        0,
                    )
                )
        total = lax.dot_general(
            jnp.concatenate(parts, 1), wt4[...], (((1,), (1,)), ((), ())), preferred_element_type=F32
        )
        total = resid[pl.ds(pl.multiple_of(chunk * 320 + 128, 64), 320), :] + (total + bias4)
        for x in range(5):
            for py in range(2):
                pieces = [
                    total[x * 64 + k * 16 : x * 64 + k * 16 + 16, py * 128 : py * 128 + C4] for k in range(4)
                ]
                line = jnp.concatenate(pieces, 1)
                for tile in range(3):
                    outs[(chunk * 5 + x) * 3 + tile, pl.ds(py, 16, stride=2), :] = line[:, tile * 128 : tile * 128 + 128]
        return 0

    lax.fori_loop(0, 4, four, 0)
    for tile in range(60):
        out[:, tile * 128 : tile * 128 + 128] = outs[tile].astype(BF)


def shards(sizes, section_input, cache_three, gain_three, bias_three, weight_three, weight_up, bias_up, cache_four,
           gain_four, weight_four, bias_four):
    vmem = pl.BlockSpec(memory_space=pltpu.VMEM)
    hbm = pl.BlockSpec(memory_space=pl.ANY)
    scratch = [
        pltpu.VMEM((ROWS, X_LANES), BF),
        pltpu.VMEM((ROWS, P_LANES), BF),
        pltpu.VMEM((2 * ROWS, Q_LANES), BF),
        pltpu.VMEM((27, C3 * C3), BF),
        pltpu.VMEM((9, C3 * C4), BF),
        pltpu.VMEM((27, C4 * C4), BF),
        pltpu.VMEM((2, EDGE), BF),
        pltpu.VMEM((2, EDGE), BF),
        pltpu.VMEM((4, 2, CORNER), BF),
        pltpu.VMEM((2, EDGE), BF),
        pltpu.VMEM((2, EDGE), BF),
        pltpu.VMEM((4, 2, CORNER), BF),
        pltpu.VMEM((ROWS, 1536), BF),
        pltpu.VMEM((ROWS, 1536), BF),
        pltpu.VMEM((ROWS, 768), BF),
        pltpu.VMEM((ROWS, 768), BF),
        pltpu.VMEM((2 * ROWS, 256), BF),
        pltpu.VMEM((2 * ROWS, 256), BF),
        pltpu.VMEM((14 * 96, 256), F32),
        pltpu.VMEM((14 * 48, 256), F32),
        pltpu.VMEM((14 * 144, 768), BF),
        pltpu.VMEM((14 * 96, 768), BF),
        pltpu.VMEM((256, 27 * 256), BF),
        pltpu.VMEM((2, 256, 1536), BF),
        pltpu.VMEM((256, 9 * 512), BF),
        pltpu.VMEM((14 * 96, 768), BF),
        pltpu.VMEM((2, 1152, 256), F32),
        pltpu.VMEM((24 * 96, 512), BF),
        pltpu.VMEM((24 * 64, 256), F32),
        pltpu.VMEM((48, Q_LANES + 512), BF),
        pltpu.VMEM((60, 32, 128), F32),
        pltpu.SemaphoreType.DMA((6,)),
        pltpu.SemaphoreType.DMA((12,)),
        pltpu.SemaphoreType.DMA((12,)),
    ]
    return pl.pallas_call(
        functools.partial(kernel, sizes),
        out_shape=jax.ShapeDtypeStruct((2 * ROWS, 2 * X_LANES // 2), BF),
        in_specs=[hbm] * 6 + [vmem] * 5,
        out_specs=vmem,
        scratch_shapes=scratch,
        compiler_params=pltpu.CompilerParams(
            collective_id=0, has_side_effects=True, vmem_limit_bytes=60 * 2**20
        ),
        name="decode",
    )(section_input, cache_three, cache_four, weight_three, weight_up, weight_four, gain_three, bias_three, bias_up,
      gain_four, bias_four)


def solution(mesh):
    sizes = (mesh.shape["row"], mesh.shape["section"], mesh.shape["col"])
    tiled = P("row", ("section", "col"))
    return jax.shard_map(
        functools.partial(shards, sizes),
        mesh=mesh,
        in_specs=(tiled, tiled, P(), P(), P(), P(), P(), tiled, P(), P(), P()),
        out_specs=tiled,
        check_vma=False,
    )
```

```python
import functools

import jax
import jax.numpy as jnp
from jax import lax
from jax.experimental import pallas as pl
from jax.experimental.pallas import tpu as pltpu
from jax.sharding import PartitionSpec as P

EPSILON = 1e-06
MESH = pl.DeviceIdType.MESH
BF = jnp.bfloat16
F32 = jnp.float32
C3 = 192
C4 = 96
ROWS = 16
COLS = 10
FRAMES = 4
BLOCK = 24
X_LANES = COLS * FRAMES * C3
P_LANES = COLS * 2 * C3
Q_LANES = 2 * COLS * 2 * C4
EDGE = X_LANES + P_LANES + Q_LANES
CORNER = 1536 + 768 + 256


def widen(value, lanes):
    pad = lanes - value.shape[1]
    return jnp.concatenate([value, jnp.zeros((value.shape[0], pad), value.dtype)], axis=1)


def norm_act(values, gain, channels):
    meansq = jnp.sum(values * values, axis=-1, keepdims=True) * (1.0 / channels)
    scaled = values * lax.rsqrt(meansq + EPSILON) * gain
    half = 0.5 * scaled
    return half + half * jnp.tanh(half)


def rounded(values):
    return values.astype(BF).astype(F32)


def by_tap(chunk, outs, stride, take):
    taps = chunk.shape[0]
    full = -(-taps // 8) * 8
    wide = jnp.concatenate([chunk, jnp.zeros((full - taps, chunk.shape[1]), chunk.dtype)], 0).astype(F32)
    pieces = []
    for start, count in take:
        stacked = jnp.stack(
            [widen(wide[:, o * stride + start : o * stride + start + count], 128) if count < 128 else
             wide[:, o * stride + start : o * stride + start + count] for o in range(outs)], 0)
        pieces.append(jnp.swapaxes(stacked, 0, 1))
    return pieces


def kernel(
    sizes,
    x_hbm, p_hbm, q_hbm, w3_hbm, wu_hbm, w4_hbm, g3_hbm, b3_hbm, bu_hbm, g4_hbm, b4_hbm,
    out,
    g3, b3, bu, g4, b4,
    xv, pv, qv, w3v, wuv, w4v,
    top, bottom, corner_send,
    from_up, from_down, corner_recv, xl, xr, pl_, pr, ql, qr,
    xs, ps, act, act_one, wt3, wtu, wt4, r3s, s4, a4, resid, qext, outs,
    load_sem, send_sem, recv_sem,
):
    row_count, section_count, col_count = sizes
    r = lax.axis_index("row")
    flat_count = section_count * col_count
    g = lax.axis_index("section") * col_count + lax.axis_index("col")
    up, down = lax.rem(r + row_count - 1, row_count), lax.rem(r + 1, row_count)
    left, right = lax.rem(g + flat_count - 1, flat_count), lax.rem(g + 1, flat_count)

    def device(row, flat):
        return {"row": row, "section": flat // col_count, "col": lax.rem(flat, col_count)}

    neighbours = [(up, left), (up, g), (up, right), (r, left), (r, right), (down, left), (down, g), (down, right)]

    loads = [
        pltpu.make_async_copy(src, dst, load_sem.at[i])
        for i, (src, dst) in enumerate(
            ((x_hbm, xv), (p_hbm, pv), (q_hbm, qv), (wu_hbm, wuv), (w4_hbm, w4v), (w3_hbm, w3v),
             (g3_hbm, g3), (b3_hbm, b3), (bu_hbm, bu), (g4_hbm, g4), (b4_hbm, b4))
        )
    ]
    for load in loads[:3]:
        load.start()

    barrier = pltpu.get_barrier_semaphore()
    for row, flat in neighbours:
        pl.semaphore_signal(barrier, inc=1, device_id=device(row, flat), device_id_type=MESH)

    for load in loads[:3]:
        load.wait()
    for buf, rows3, rows4 in ((top, (0, 2), (0, 2)), (bottom, (ROWS - 2, ROWS), (2 * ROWS - 2, 2 * ROWS))):
        buf[:, 0:X_LANES] = xv[rows3[0] : rows3[1], :]
        buf[:, X_LANES : X_LANES + P_LANES] = pv[rows3[0] : rows3[1], :]
        buf[:, X_LANES + P_LANES : EDGE] = qv[rows4[0] : rows4[1], :]
    for index, (rows3, rows4, high) in enumerate(
        (
            ((0, 2), (0, 2), False),
            ((0, 2), (0, 2), True),
            ((ROWS - 2, ROWS), (2 * ROWS - 2, 2 * ROWS), False),
            ((ROWS - 2, ROWS), (2 * ROWS - 2, 2 * ROWS), True),
        )
    ):
        xo, po, qo = (X_LANES - 1536, P_LANES - 768, Q_LANES - 256) if high else (0, 0, 0)
        corner_send[index, :, 0:1536] = xv[rows3[0] : rows3[1], xo : xo + 1536]
        corner_send[index, :, 1536:2304] = pv[rows3[0] : rows3[1], po : po + 768]
        corner_send[index, :, 2304:2560] = qv[rows4[0] : rows4[1], qo : qo + 256]

    for load in loads[3:]:
        load.start()

    pl.semaphore_wait(barrier, len(neighbours))

    plan = [
        (top, from_down, up, g),
        (bottom, from_up, down, g),
        (corner_send.at[0], corner_recv.at[3], up, left),
        (corner_send.at[1], corner_recv.at[2], up, right),
        (corner_send.at[2], corner_recv.at[1], down, left),
        (corner_send.at[3], corner_recv.at[0], down, right),
        (xv.at[:, 0:1536], xr, r, left),
        (xv.at[:, X_LANES - 1536 : X_LANES], xl, r, right),
        (pv.at[:, 0:768], pr, r, left),
        (pv.at[:, P_LANES - 768 : P_LANES], pl_, r, right),
        (qv.at[:, 0:256], qr, r, left),
        (qv.at[:, Q_LANES - 256 : Q_LANES], ql, r, right),
    ]
    copies = [
        pltpu.make_async_remote_copy(
            src_ref=src,
            dst_ref=dst,
            send_sem=send_sem.at[i],
            recv_sem=recv_sem.at[i],
            device_id=device(row, flat),
            device_id_type=MESH,
        )
        for i, (src, dst, row, flat) in enumerate(plan)
    ]
    for copy in copies:
        copy.start()

    wt3[...] = jnp.zeros_like(wt3)
    wtu[...] = jnp.zeros_like(wtu)
    wt4[...] = jnp.zeros_like(wt4)
    xs[...] = jnp.zeros_like(xs)
    ps[...] = jnp.zeros_like(ps)
    a4[...] = jnp.zeros_like(a4)
    r3s[0:96, :] = jnp.zeros((96, 768), BF)
    r3s[13 * 96 : 14 * 96, :] = jnp.zeros((96, 768), BF)

    loads[3].wait()

    def up_weights(group, _):
        chunk = wuv[:, pl.ds(pl.multiple_of(group * 16 * C3, 128), 16 * C3)]
        pieces = by_tap(chunk, 16, C3, ((0, 128), (128, 64)))
        for half, taps in enumerate(pieces):
            tap = [[taps[3 * dy + dx] for dx in range(3)] for dy in range(3)]
            across = [
                {(0, 0): line[0], (0, 1): line[1] + line[2], (1, 1): line[0] + line[1], (1, 2): line[2]} for line in tap
            ]
            for (px, dx), _first in across[0].items():
                vals = [line[(px, dx)] for line in across]
                for py, slots in enumerate(((vals[0], vals[1] + vals[2]), (vals[0] + vals[1], vals[2]))):
                    for slot, val in enumerate(slots):
                        lane = dx * 512 + slot * 256 + half * 128
                        wtu[py, pl.ds(pl.multiple_of(px * 128 + group * 16, 16), 16), lane : lane + 128] = val.astype(BF)
        return 0

    lax.fori_loop(0, 6, up_weights, 0)

    loads[4].wait()

    def four_weights(group, _):
        chunk = w4v[:, pl.ds(pl.multiple_of(group * 16 * C4, 128), 16 * C4)]
        (taps,) = by_tap(chunk, 16, C4, ((0, C4),))
        for t in range(3):
            for dx in range(3):
                for dy in range(3):
                    val = taps[9 * t + 3 * dy + dx].astype(BF)
                    for py in range(2):
                        lane = (t * 3 + dx) * 512 + (dy + py) * 128
                        wt4[pl.ds(pl.multiple_of(py * 128 + group * 16, 16), 16), lane : lane + 128] = val
        return 0

    lax.fori_loop(0, 6, four_weights, 0)

    loads[5].wait()

    def three_weights(group, _):
        chunk = w3v[:, pl.ds(pl.multiple_of(group * 16 * C3, 128), 16 * C3)]
        pieces = by_tap(chunk, 16, C3, ((0, 128), (128, 64)))
        for half, taps in enumerate(pieces):
            for t in range(3):
                for dx in range(3):
                    for dy in range(3):
                        lane = ((t * 3 + dx) * 3 + dy) * 256 + half * 128
                        wt3[pl.ds(pl.multiple_of(group * 16, 16), 16), lane : lane + 128] = taps[
                            9 * t + 3 * dy + dx
                        ].astype(BF)
        return 0

    lax.fori_loop(0, 12, three_weights, 0)

    for load in loads[6:]:
        load.wait()
    for copy in copies:
        copy.wait()

    at_top, at_bottom, at_left, at_right = r == 0, r == row_count - 1, g == 0, g == flat_count - 1

    def keep(value, outside):
        return jnp.where(outside, jnp.zeros_like(value), value)

    for je in range(14):
        j = je - 2
        for frames, buf, main, low, high, edge_base, corner_base in (
            (FRAMES, xs, xv, xl, xr, 0, 0),
            (2, ps, pv, pl_, pr, X_LANES, 1536),
        ):
            wide = frames * C3
            if j < 0:
                side = at_left
                mid = keep(low[:, je * wide : (je + 1) * wide].astype(F32), side)
                above = corner_recv[0, :, corner_base + je * wide : corner_base + (je + 1) * wide].astype(F32)
                below = corner_recv[2, :, corner_base + je * wide : corner_base + (je + 1) * wide].astype(F32)
            elif j >= COLS:
                side = at_right
                jr = j - COLS
                mid = keep(high[:, jr * wide : (jr + 1) * wide].astype(F32), side)
                above = corner_recv[1, :, corner_base + jr * wide : corner_base + (jr + 1) * wide].astype(F32)
                below = corner_recv[3, :, corner_base + jr * wide : corner_base + (jr + 1) * wide].astype(F32)
            else:
                side = jnp.bool_(False)
                mid = main[:, j * wide : (j + 1) * wide].astype(F32)
                above = from_up[:, edge_base + j * wide : edge_base + (j + 1) * wide].astype(F32)
                below = from_down[:, edge_base + j * wide : edge_base + (j + 1) * wide].astype(F32)
            above = keep(above, jnp.logical_or(side, at_top))
            below = keep(below, jnp.logical_or(side, at_bottom))
            for k in range(frames):
                base = (je * frames + k) * BLOCK
                lanes = slice(k * C3, (k + 1) * C3)
                buf[base : base + 16, 0:C3] = mid[:, lanes]
                buf[base + 16 : base + 18, 0:C3] = below[:, lanes]
                buf[base + 22 : base + 24, 0:C3] = above[:, lanes]

    gain3 = widen(g3[...].reshape(1, C3), 256)
    bias3 = widen(b3[...].reshape(1, C3), 256)

    def build(je, _):
        raw = xs[pl.ds(pl.multiple_of(je * 96, 32), 96), :]
        new = norm_act(raw, gain3, C3).reshape(4, BLOCK, 256)
        old = ps[pl.ds(pl.multiple_of(je * 48, 16), 48), :].reshape(2, BLOCK, 256)
        frames = jnp.concatenate([old, new], 0)
        for slot, shift in enumerate((1, 0, BLOCK - 1)):
            moved = pltpu.roll(frames, shift, axis=1) if shift else frames
            lanes = slice(slot * 256, (slot + 1) * 256)
            act[pl.ds(pl.multiple_of(je * 144, 16), 144), lanes] = moved.reshape(144, 256).astype(BF)
            act_one[pl.ds(pl.multiple_of(je * 96, 32), 96), lanes] = moved[1:5].reshape(96, 256).astype(BF)
        return 0

    lax.fori_loop(0, 14, build, 0)

    def three(chunk, _):
        parts = []
        for t in range(3):
            for dx in range(3):
                rows = []
                for j in range(4):
                    je = chunk * 4 + j + dx
                    if t == 1:
                        rows.append(act_one[pl.ds(pl.multiple_of(je * 96, 32), 96), :])
                    else:
                        rows.append(act[pl.ds(pl.multiple_of(je * 144 + 24 * t, 16), 96), :])
                parts.append(jnp.concatenate(rows, 0))
        total = lax.dot_general(
            jnp.concatenate(parts, 1), wt3[...], (((1,), (1,)), ((), ())), preferred_element_type=F32
        )
        total = xs[pl.ds(pl.multiple_of(chunk * 384 + 96, 32), 384), :] + (total + bias3)
        total = total.reshape(16, BLOCK, 256)
        blk = lax.broadcasted_iota(jnp.int32, (16, BLOCK, 256), 0) + chunk * 16
        rr = lax.broadcasted_iota(jnp.int32, (16, BLOCK, 256), 1)
        lowest = jnp.where(at_left, 4, 0)
        highest = jnp.where(at_right, 44, 48)
        up_row = jnp.where(at_top, 23, -1)
        down_row = jnp.where(at_bottom, 16, -1)
        inside = (blk >= lowest) & (blk < highest) & (rr != up_row) & (rr != down_row)
        total = rounded(jnp.where(inside, total, 0.0))
        for slot, shift in enumerate((1, 0, BLOCK - 1)):
            moved = pltpu.roll(total, shift, axis=1) if shift else total
            r3s[pl.ds(pl.multiple_of(chunk * 384 + 96, 32), 384), slot * 256 : (slot + 1) * 256] = moved.reshape(
                384, 256
            ).astype(BF)
        return 0

    lax.fori_loop(0, 3, three, 0)

    bias_u = bu[...].reshape(1, C4)
    bias_u = jnp.concatenate([widen(bias_u, 128)] * 2, 1)

    def upsample(chunk, _):
        for py in range(2):
            parts = [
                r3s[pl.ds(pl.multiple_of(chunk * 384 + dx * 96, 32), 384), py * 256 : py * 256 + 512]
                for dx in range(3)
            ]
            total = lax.dot_general(
                jnp.concatenate(parts, 1), wtu[py], (((1,), (1,)), ((), ())), preferred_element_type=F32
            )
            s4[py, pl.ds(pl.multiple_of(chunk * 384, 128), 384), :] = total + bias_u
        return 0

    lax.fori_loop(0, 3, upsample, 0)

    gain4 = widen(g4[...].reshape(1, C4), 128)

    def four_in(jj, _):
        for px in range(2):
            acts = []
            at = jj * 2 + px
            for py in range(2):
                value = rounded(s4[py, pl.ds(pl.multiple_of(jj * 96, 32), 96), px * 128 : px * 128 + 128])
                shaped = value.reshape(4, BLOCK, 128)
                resid[pl.ds(pl.multiple_of(at * 64, 64), 64), py * 128 : py * 128 + 128] = shaped[:, 0:16].reshape(64, 128)
                active = norm_act(value, gain4, C4).reshape(4, BLOCK, 128)
                rr = lax.broadcasted_iota(jnp.int32, (4, BLOCK, 128), 1)
                line = jnp.where(at_bottom, 16, -1) if py == 0 else jnp.where(at_top, 23, -1)
                column = jnp.logical_or(jnp.logical_and(at_left, at < 2), jnp.logical_and(at_right, at > 21))
                line = jnp.where(column, -2, line)
                active = jnp.where(jnp.logical_or(rr == line, line == -2), 0.0, active)
                acts.append(active)
            slots = (
                pltpu.roll(acts[1], 1, axis=1),
                acts[0],
                acts[1],
                pltpu.roll(acts[0], BLOCK - 1, axis=1),
            )
            for slot, value in enumerate(slots):
                a4[pl.ds(pl.multiple_of(at * 96 + 32, 32), 64), slot * 128 : slot * 128 + 128] = (
                    value[:, 0:16].reshape(64, 128).astype(BF)
                )
        return 0

    lax.fori_loop(0, 12, four_in, 0)

    qext[...] = jnp.zeros_like(qext)
    edge_q = X_LANES + P_LANES
    qext[0:32, 256 : 256 + Q_LANES] = qv[...]
    qext[0:32, 0:256] = keep(ql[...], at_left)
    qext[0:32, 256 + Q_LANES : 512 + Q_LANES] = keep(qr[...], at_right)
    for base, edge, outside, low_corner, high_corner in (
        (32, from_up, at_top, 0, 1),
        (40, from_down, at_bottom, 2, 3),
    ):
        qext[base : base + 2, 256 : 256 + Q_LANES] = keep(edge[:, edge_q:EDGE], outside)
        qext[base : base + 2, 0:256] = keep(corner_recv[low_corner, :, 2304:2560], jnp.logical_or(outside, at_left))
        qext[base : base + 2, 256 + Q_LANES : 512 + Q_LANES] = keep(
            corner_recv[high_corner, :, 2304:2560], jnp.logical_or(outside, at_right)
        )
    want = lax.broadcasted_iota(jnp.int32, (64, 48), 0)
    have = lax.broadcasted_iota(jnp.int32, (64, 48), 1)
    slot = want >> 4
    i = want & 15
    source = jnp.where(
        slot == 0,
        jnp.where(i == 0, 33, 2 * i - 1),
        jnp.where(slot == 1, 2 * i, jnp.where(slot == 2, 2 * i + 1, jnp.where(i == 15, 40, 2 * i + 2))),
    )
    pick = jnp.where(source == have, 1.0, 0.0).astype(BF)
    for xe in range(22):
        start = 64 + xe * 192
        low = start // 128 * 128
        picked = jnp.dot(pick, qext[:, low : low + 256], preferred_element_type=F32)
        for t in range(2):
            off = start - low + t * C4
            piece = picked[:, off : off + C4].astype(BF)
            for s in range(4):
                a4[(xe + 1) * 96 + t * 16 : (xe + 1) * 96 + t * 16 + 16, s * 128 : s * 128 + C4] = piece[
                    s * 16 : s * 16 + 16
                ]

    bias4 = widen(b4[...].reshape(1, C4), 128)
    bias4 = jnp.concatenate([bias4, bias4], 1)

    def four(chunk, _):
        parts = []
        for t in range(3):
            for dx in range(3):
                parts.append(
                    jnp.concatenate(
                        [
                            a4[pl.ds(pl.multiple_of((chunk * 5 + x + 1 + dx) * 96 + t * 16, 16), 64), :]
                            for x in range(5)
                        ],
                        0,
                    )
                )
        total = lax.dot_general(
            jnp.concatenate(parts, 1), wt4[...], (((1,), (1,)), ((), ())), preferred_element_type=F32
        )
        total = resid[pl.ds(pl.multiple_of(chunk * 320 + 128, 64), 320), :] + (total + bias4)
        for x in range(5):
            for py in range(2):
                pieces = [
                    total[x * 64 + k * 16 : x * 64 + k * 16 + 16, py * 128 : py * 128 + C4] for k in range(4)
                ]
                line = jnp.concatenate(pieces, 1)
                for tile in range(3):
                    outs[(chunk * 5 + x) * 3 + tile, pl.ds(py, 16, stride=2), :] = line[:, tile * 128 : tile * 128 + 128]
        return 0

    lax.fori_loop(0, 4, four, 0)
    for tile in range(60):
        out[:, tile * 128 : tile * 128 + 128] = outs[tile].astype(BF)


def shards(sizes, section_input, cache_three, gain_three, bias_three, weight_three, weight_up, bias_up, cache_four,
           gain_four, weight_four, bias_four):
    vmem = pl.BlockSpec(memory_space=pltpu.VMEM)
    hbm = pl.BlockSpec(memory_space=pl.ANY)
    scratch = [
        pltpu.VMEM((C3,), F32),
        pltpu.VMEM((C3,), F32),
        pltpu.VMEM((C4,), F32),
        pltpu.VMEM((C4,), F32),
        pltpu.VMEM((C4,), F32),
        pltpu.VMEM((ROWS, X_LANES), BF),
        pltpu.VMEM((ROWS, P_LANES), BF),
        pltpu.VMEM((2 * ROWS, Q_LANES), BF),
        pltpu.VMEM((27, C3 * C3), BF),
        pltpu.VMEM((9, C3 * C4), BF),
        pltpu.VMEM((27, C4 * C4), BF),
        pltpu.VMEM((2, EDGE), BF),
        pltpu.VMEM((2, EDGE), BF),
        pltpu.VMEM((4, 2, CORNER), BF),
        pltpu.VMEM((2, EDGE), BF),
        pltpu.VMEM((2, EDGE), BF),
        pltpu.VMEM((4, 2, CORNER), BF),
        pltpu.VMEM((ROWS, 1536), BF),
        pltpu.VMEM((ROWS, 1536), BF),
        pltpu.VMEM((ROWS, 768), BF),
        pltpu.VMEM((ROWS, 768), BF),
        pltpu.VMEM((2 * ROWS, 256), BF),
        pltpu.VMEM((2 * ROWS, 256), BF),
        pltpu.VMEM((14 * 96, 256), F32),
        pltpu.VMEM((14 * 48, 256), F32),
        pltpu.VMEM((14 * 144, 768), BF),
        pltpu.VMEM((14 * 96, 768), BF),
        pltpu.VMEM((256, 27 * 256), BF),
        pltpu.VMEM((2, 256, 1536), BF),
        pltpu.VMEM((256, 9 * 512), BF),
        pltpu.VMEM((14 * 96, 768), BF),
        pltpu.VMEM((2, 1152, 256), F32),
        pltpu.VMEM((24 * 96, 512), BF),
        pltpu.VMEM((24 * 64, 256), F32),
        pltpu.VMEM((48, Q_LANES + 512), BF),
        pltpu.VMEM((60, 32, 128), F32),
        pltpu.SemaphoreType.DMA((11,)),
        pltpu.SemaphoreType.DMA((12,)),
        pltpu.SemaphoreType.DMA((12,)),
    ]
    return pl.pallas_call(
        functools.partial(kernel, sizes),
        out_shape=jax.ShapeDtypeStruct((2 * ROWS, 2 * X_LANES // 2), BF),
        in_specs=[hbm] * 11,
        out_specs=vmem,
        scratch_shapes=scratch,
        compiler_params=pltpu.CompilerParams(
            collective_id=0, has_side_effects=True, vmem_limit_bytes=60 * 2**20
        ),
        name="decode",
    )(section_input, cache_three, cache_four, weight_three, weight_up, weight_four, gain_three, bias_three, bias_up,
      gain_four, bias_four)


def solution(mesh):
    sizes = (mesh.shape["row"], mesh.shape["section"], mesh.shape["col"])
    tiled = P("row", ("section", "col"))
    return jax.shard_map(
        functools.partial(shards, sizes),
        mesh=mesh,
        in_specs=(tiled, tiled, P(), P(), P(), P(), P(), tiled, P(), P(), P()),
        out_specs=tiled,
        check_vma=False,
    )
```

```python
import functools

import jax
import jax.numpy as jnp
from jax import lax
from jax.experimental import pallas as pl
from jax.experimental.pallas import tpu as pltpu
from jax.sharding import PartitionSpec as P

EPSILON = 1e-06
MESH = pl.DeviceIdType.MESH
BF = jnp.bfloat16
F32 = jnp.float32
C3 = 192
C4 = 96
ROWS = 16
COLS = 10
FRAMES = 4
BLOCK = 24
X_LANES = COLS * FRAMES * C3
P_LANES = COLS * 2 * C3
Q_LANES = 2 * COLS * 2 * C4
EDGE = X_LANES + P_LANES + Q_LANES
CORNER = 1536 + 768 + 256


def widen(value, lanes):
    pad = lanes - value.shape[1]
    return jnp.concatenate([value, jnp.zeros((value.shape[0], pad), value.dtype)], axis=1)


def norm_act(values, gain, channels):
    meansq = jnp.sum(values * values, axis=-1, keepdims=True) * (1.0 / channels)
    scaled = values * lax.rsqrt(meansq + EPSILON) * gain
    half = 0.5 * scaled
    return half + half * jnp.tanh(half)


def rounded(values):
    return values.astype(BF).astype(F32)


def by_tap(chunk, outs, stride, take):
    taps = chunk.shape[0]
    full = -(-taps // 8) * 8
    wide = jnp.concatenate([chunk, jnp.zeros((full - taps, chunk.shape[1]), chunk.dtype)], 0).astype(F32)
    pieces = []
    for start, count in take:
        stacked = jnp.stack(
            [widen(wide[:, o * stride + start : o * stride + start + count], 128) if count < 128 else
             wide[:, o * stride + start : o * stride + start + count] for o in range(outs)], 0)
        pieces.append(jnp.swapaxes(stacked, 0, 1))
    return pieces


def kernel(
    sizes,
    x_hbm, p_hbm, q_hbm, w3_hbm, wu_hbm, w4_hbm, g3_hbm, b3_hbm, bu_hbm, g4_hbm, b4_hbm,
    out,
    g3, b3, bu, g4, b4,
    xv, pv, qv, w3v, wuv, w4v,
    top, bottom, corner_send,
    from_up, from_down, corner_recv, xl, xr, pl_, pr, ql, qr,
    xs, ps, an, act, act_one, wt3, wtu, wt4, r3s, s4, a4, resid, qext, outs,
    load_sem, send_sem, recv_sem,
):
    row_count, section_count, col_count = sizes
    r = lax.axis_index("row")
    flat_count = section_count * col_count
    g = lax.axis_index("section") * col_count + lax.axis_index("col")
    up, down = lax.rem(r + row_count - 1, row_count), lax.rem(r + 1, row_count)
    left, right = lax.rem(g + flat_count - 1, flat_count), lax.rem(g + 1, flat_count)

    def device(row, flat):
        return {"row": row, "section": flat // col_count, "col": lax.rem(flat, col_count)}

    at_top, at_bottom, at_left, at_right = r == 0, r == row_count - 1, g == 0, g == flat_count - 1
    has_up, has_down, has_left, has_right = r > 0, r < row_count - 1, g > 0, g < flat_count - 1
    up_left, up_right = jnp.logical_and(has_up, has_left), jnp.logical_and(has_up, has_right)
    down_left, down_right = jnp.logical_and(has_down, has_left), jnp.logical_and(has_down, has_right)

    neighbours = [
        (up, left, up_left), (up, g, has_up), (up, right, up_right), (r, left, has_left), (r, right, has_right),
        (down, left, down_left), (down, g, has_down), (down, right, down_right),
    ]
    count_rows = jnp.where(at_top, 0, 1) + jnp.where(at_bottom, 0, 1)
    count_cols = jnp.where(at_left, 0, 1) + jnp.where(at_right, 0, 1)

    loads = [
        pltpu.make_async_copy(src, dst, load_sem.at[i])
        for i, (src, dst) in enumerate(
            ((x_hbm, xv), (p_hbm, pv), (q_hbm, qv), (wu_hbm, wuv), (w4_hbm, w4v), (w3_hbm, w3v),
             (g3_hbm, g3), (b3_hbm, b3), (bu_hbm, bu), (g4_hbm, g4), (b4_hbm, b4))
        )
    ]
    for load in loads[:3]:
        load.start()

    barrier = pltpu.get_barrier_semaphore()
    for row, flat, there in neighbours:

        @pl.when(there)
        def _(row=row, flat=flat):
            pl.semaphore_signal(barrier, inc=1, device_id=device(row, flat), device_id_type=MESH)

    for load in loads[:3]:
        load.wait()
    for buf, rows3, rows4 in ((top, (0, 2), (0, 2)), (bottom, (ROWS - 2, ROWS), (2 * ROWS - 2, 2 * ROWS))):
        buf[:, 0:X_LANES] = xv[rows3[0] : rows3[1], :]
        buf[:, X_LANES : X_LANES + P_LANES] = pv[rows3[0] : rows3[1], :]
        buf[:, X_LANES + P_LANES : EDGE] = qv[rows4[0] : rows4[1], :]
    for index, (rows3, rows4, high) in enumerate(
        (
            ((0, 2), (0, 2), False),
            ((0, 2), (0, 2), True),
            ((ROWS - 2, ROWS), (2 * ROWS - 2, 2 * ROWS), False),
            ((ROWS - 2, ROWS), (2 * ROWS - 2, 2 * ROWS), True),
        )
    ):
        xo, po, qo = (X_LANES - 1536, P_LANES - 768, Q_LANES - 256) if high else (0, 0, 0)
        corner_send[index, :, 0:1536] = xv[rows3[0] : rows3[1], xo : xo + 1536]
        corner_send[index, :, 1536:2304] = pv[rows3[0] : rows3[1], po : po + 768]
        corner_send[index, :, 2304:2560] = qv[rows4[0] : rows4[1], qo : qo + 256]

    for load in loads[3:]:
        load.start()

    pl.semaphore_wait(barrier, (1 + count_rows) * (1 + count_cols) - 1)

    plan = [
        (top, from_down, up, g, has_up, has_down),
        (bottom, from_up, down, g, has_down, has_up),
        (xv.at[:, 0:1536], xr, r, left, has_left, has_right),
        (xv.at[:, X_LANES - 1536 : X_LANES], xl, r, right, has_right, has_left),
        (pv.at[:, 0:768], pr, r, left, has_left, has_right),
        (pv.at[:, P_LANES - 768 : P_LANES], pl_, r, right, has_right, has_left),
        (corner_send.at[0], corner_recv.at[3], up, left, up_left, down_right),
        (corner_send.at[1], corner_recv.at[2], up, right, up_right, down_left),
        (corner_send.at[2], corner_recv.at[1], down, left, down_left, up_right),
        (corner_send.at[3], corner_recv.at[0], down, right, down_right, up_left),
        (qv.at[:, 0:256], qr, r, left, has_left, has_right),
        (qv.at[:, Q_LANES - 256 : Q_LANES], ql, r, right, has_right, has_left),
    ]
    copies = [
        (
            pltpu.make_async_remote_copy(
                src_ref=src,
                dst_ref=dst,
                send_sem=send_sem.at[i],
                recv_sem=recv_sem.at[i],
                device_id=device(row, flat),
                device_id_type=MESH,
            ),
            sends,
            gets,
        )
        for i, (src, dst, row, flat, sends, gets) in enumerate(plan)
    ]
    for copy, sends, _gets in copies:

        @pl.when(sends)
        def _(copy=copy):
            copy.start()

    wt3[...] = jnp.zeros_like(wt3)
    wtu[...] = jnp.zeros_like(wtu)
    wt4[...] = jnp.zeros_like(wt4)
    xs[...] = jnp.zeros_like(xs)
    ps[...] = jnp.zeros_like(ps)
    a4[...] = jnp.zeros_like(a4)
    r3s[0:96, :] = jnp.zeros((96, 768), BF)
    r3s[13 * 96 : 14 * 96, :] = jnp.zeros((96, 768), BF)

    loads[3].wait()

    def up_weights(group, _):
        chunk = wuv[:, pl.ds(pl.multiple_of(group * 16 * C3, 128), 16 * C3)]
        pieces = by_tap(chunk, 16, C3, ((0, 128), (128, 64)))
        for half, taps in enumerate(pieces):
            tap = [[taps[3 * dy + dx] for dx in range(3)] for dy in range(3)]
            across = [
                {(0, 0): line[0], (0, 1): line[1] + line[2], (1, 1): line[0] + line[1], (1, 2): line[2]} for line in tap
            ]
            for (px, dx), _first in across[0].items():
                vals = [line[(px, dx)] for line in across]
                for py, slots in enumerate(((vals[0], vals[1] + vals[2]), (vals[0] + vals[1], vals[2]))):
                    for slot, val in enumerate(slots):
                        lane = dx * 512 + slot * 256 + half * 128
                        wtu[py, pl.ds(pl.multiple_of(px * 128 + group * 16, 16), 16), lane : lane + 128] = val.astype(BF)
        return 0

    lax.fori_loop(0, 6, up_weights, 0)

    loads[4].wait()

    def four_weights(group, _):
        chunk = w4v[:, pl.ds(pl.multiple_of(group * 16 * C4, 128), 16 * C4)]
        (taps,) = by_tap(chunk, 16, C4, ((0, C4),))
        for t in range(3):
            for dx in range(3):
                for dy in range(3):
                    val = taps[9 * t + 3 * dy + dx].astype(BF)
                    for py in range(2):
                        lane = (t * 3 + dx) * 512 + (dy + py) * 128
                        wt4[pl.ds(pl.multiple_of(py * 128 + group * 16, 16), 16), lane : lane + 128] = val
        return 0

    lax.fori_loop(0, 6, four_weights, 0)

    loads[5].wait()

    def three_weights(group, _):
        chunk = w3v[:, pl.ds(pl.multiple_of(group * 16 * C3, 128), 16 * C3)]
        pieces = by_tap(chunk, 16, C3, ((0, 128), (128, 64)))
        for half, taps in enumerate(pieces):
            for t in range(3):
                for dx in range(3):
                    for dy in range(3):
                        lane = ((t * 3 + dx) * 3 + dy) * 256 + half * 128
                        wt3[pl.ds(pl.multiple_of(group * 16, 16), 16), lane : lane + 128] = taps[
                            9 * t + 3 * dy + dx
                        ].astype(BF)
        return 0

    lax.fori_loop(0, 12, three_weights, 0)

    for load in loads[6:]:
        load.wait()

    qext[...] = jnp.zeros_like(qext)
    qext[0:32, 256 : 256 + Q_LANES] = qv[...]
    gain3 = widen(g3[...].reshape(1, C3), 256)
    bias3 = widen(b3[...].reshape(1, C3), 256)

    for je in range(2, 2 + COLS):
        for frames, buf, main in ((FRAMES, xs, xv), (2, ps, pv)):
            wide = frames * C3
            mid = main[:, (je - 2) * wide : (je - 1) * wide].astype(F32)
            for k in range(frames):
                base = (je * frames + k) * BLOCK
                buf[base : base + 16, 0:C3] = mid[:, k * C3 : (k + 1) * C3]

    def own(j, _):
        rows = [xs[pl.ds(pl.multiple_of(j * 96 + 192 + k * BLOCK, 8), 16), :] for k in range(FRAMES)]
        an[pl.ds(pl.multiple_of(j * 64, 64), 64), :] = norm_act(jnp.concatenate(rows, 0), gain3, C3)
        return 0

    lax.fori_loop(0, COLS, own, 0)

    for copy, sends, gets in copies:

        @pl.when(gets)
        def _(copy=copy):
            copy.wait_recv()

    def keep(value, outside):
        return jnp.where(outside, jnp.zeros_like(value), value)

    for je in range(14):
        j = je - 2
        for frames, buf, main, low, high, edge_base, corner_base in (
            (FRAMES, xs, xv, xl, xr, 0, 0),
            (2, ps, pv, pl_, pr, X_LANES, 1536),
        ):
            wide = frames * C3
            if j < 0:
                side = at_left
                mid = keep(low[:, je * wide : (je + 1) * wide].astype(F32), side)
                above = corner_recv[0, :, corner_base + je * wide : corner_base + (je + 1) * wide].astype(F32)
                below = corner_recv[2, :, corner_base + je * wide : corner_base + (je + 1) * wide].astype(F32)
            elif j >= COLS:
                side = at_right
                jr = j - COLS
                mid = keep(high[:, jr * wide : (jr + 1) * wide].astype(F32), side)
                above = corner_recv[1, :, corner_base + jr * wide : corner_base + (jr + 1) * wide].astype(F32)
                below = corner_recv[3, :, corner_base + jr * wide : corner_base + (jr + 1) * wide].astype(F32)
            else:
                side = jnp.bool_(False)
                mid = None
                above = from_up[:, edge_base + j * wide : edge_base + (j + 1) * wide].astype(F32)
                below = from_down[:, edge_base + j * wide : edge_base + (j + 1) * wide].astype(F32)
            above = keep(above, jnp.logical_or(side, at_top))
            below = keep(below, jnp.logical_or(side, at_bottom))
            for k in range(frames):
                base = (je * frames + k) * BLOCK
                lanes = slice(k * C3, (k + 1) * C3)
                if mid is not None:
                    buf[base : base + 16, 0:C3] = mid[:, lanes]
                buf[base + 16 : base + 18, 0:C3] = below[:, lanes]
                buf[base + 22 : base + 24, 0:C3] = above[:, lanes]

    def place(je, new):
        old = ps[pl.ds(pl.multiple_of(je * 48, 16), 48), :].reshape(2, BLOCK, 256)
        frames = jnp.concatenate([old, new], 0)
        for slot, shift in enumerate((1, 0, BLOCK - 1)):
            moved = pltpu.roll(frames, shift, axis=1) if shift else frames
            lanes = slice(slot * 256, (slot + 1) * 256)
            act[pl.ds(pl.multiple_of(je * 144, 16), 144), lanes] = moved.reshape(144, 256).astype(BF)
            act_one[pl.ds(pl.multiple_of(je * 96, 32), 96), lanes] = moved[1:5].reshape(96, 256).astype(BF)

    def side_build(i, _):
        je = i + (i // 2) * 10
        raw = xs[pl.ds(pl.multiple_of(je * 96, 32), 96), :]
        place(je, norm_act(raw, gain3, C3).reshape(4, BLOCK, 256))
        return 0

    def own_build(j, _):
        je = j + 2
        rows = [xs[pl.ds(pl.multiple_of(je * 96 + k * BLOCK + 16, 8), 8), :] for k in range(FRAMES)]
        edge = norm_act(jnp.concatenate(rows, 0), gain3, C3).reshape(4, 8, 256)
        main = an[pl.ds(pl.multiple_of(j * 64, 64), 64), :].reshape(4, 16, 256)
        place(je, jnp.concatenate([main, edge], 1))
        return 0

    lax.fori_loop(0, 4, side_build, 0)
    lax.fori_loop(0, COLS, own_build, 0)

    def three(chunk, _):
        parts = []
        for t in range(3):
            for dx in range(3):
                rows = []
                for j in range(4):
                    je = chunk * 4 + j + dx
                    if t == 1:
                        rows.append(act_one[pl.ds(pl.multiple_of(je * 96, 32), 96), :])
                    else:
                        rows.append(act[pl.ds(pl.multiple_of(je * 144 + 24 * t, 16), 96), :])
                parts.append(jnp.concatenate(rows, 0))
        total = lax.dot_general(
            jnp.concatenate(parts, 1), wt3[...], (((1,), (1,)), ((), ())), preferred_element_type=F32
        )
        total = xs[pl.ds(pl.multiple_of(chunk * 384 + 96, 32), 384), :] + (total + bias3)
        total = total.reshape(16, BLOCK, 256)
        blk = lax.broadcasted_iota(jnp.int32, (16, BLOCK, 256), 0) + chunk * 16
        rr = lax.broadcasted_iota(jnp.int32, (16, BLOCK, 256), 1)
        lowest = jnp.where(at_left, 4, 0)
        highest = jnp.where(at_right, 44, 48)
        up_row = jnp.where(at_top, 23, -1)
        down_row = jnp.where(at_bottom, 16, -1)
        inside = (blk >= lowest) & (blk < highest) & (rr != up_row) & (rr != down_row)
        total = rounded(jnp.where(inside, total, 0.0))
        for slot, shift in enumerate((1, 0, BLOCK - 1)):
            moved = pltpu.roll(total, shift, axis=1) if shift else total
            r3s[pl.ds(pl.multiple_of(chunk * 384 + 96, 32), 384), slot * 256 : (slot + 1) * 256] = moved.reshape(
                384, 256
            ).astype(BF)
        return 0

    lax.fori_loop(0, 3, three, 0)

    bias_u = bu[...].reshape(1, C4)
    bias_u = jnp.concatenate([widen(bias_u, 128)] * 2, 1)

    def upsample(chunk, _):
        for py in range(2):
            parts = [
                r3s[pl.ds(pl.multiple_of(chunk * 384 + dx * 96, 32), 384), py * 256 : py * 256 + 512]
                for dx in range(3)
            ]
            total = lax.dot_general(
                jnp.concatenate(parts, 1), wtu[py], (((1,), (1,)), ((), ())), preferred_element_type=F32
            )
            s4[py, pl.ds(pl.multiple_of(chunk * 384, 128), 384), :] = total + bias_u
        return 0

    lax.fori_loop(0, 3, upsample, 0)

    gain4 = widen(g4[...].reshape(1, C4), 128)

    def four_in(jj, _):
        for px in range(2):
            acts = []
            at = jj * 2 + px
            for py in range(2):
                value = rounded(s4[py, pl.ds(pl.multiple_of(jj * 96, 32), 96), px * 128 : px * 128 + 128])
                shaped = value.reshape(4, BLOCK, 128)
                resid[pl.ds(pl.multiple_of(at * 64, 64), 64), py * 128 : py * 128 + 128] = shaped[:, 0:16].reshape(64, 128)
                active = norm_act(value, gain4, C4).reshape(4, BLOCK, 128)
                rr = lax.broadcasted_iota(jnp.int32, (4, BLOCK, 128), 1)
                line = jnp.where(at_bottom, 16, -1) if py == 0 else jnp.where(at_top, 23, -1)
                column = jnp.logical_or(jnp.logical_and(at_left, at < 2), jnp.logical_and(at_right, at > 21))
                line = jnp.where(column, -2, line)
                active = jnp.where(jnp.logical_or(rr == line, line == -2), 0.0, active)
                acts.append(active)
            slots = (
                pltpu.roll(acts[1], 1, axis=1),
                acts[0],
                acts[1],
                pltpu.roll(acts[0], BLOCK - 1, axis=1),
            )
            for slot, value in enumerate(slots):
                a4[pl.ds(pl.multiple_of(at * 96 + 32, 32), 64), slot * 128 : slot * 128 + 128] = (
                    value[:, 0:16].reshape(64, 128).astype(BF)
                )
        return 0

    lax.fori_loop(0, 12, four_in, 0)

    edge_q = X_LANES + P_LANES
    qext[0:32, 0:256] = keep(ql[...], at_left)
    qext[0:32, 256 + Q_LANES : 512 + Q_LANES] = keep(qr[...], at_right)
    for base, edge, outside, low_corner, high_corner in (
        (32, from_up, at_top, 0, 1),
        (40, from_down, at_bottom, 2, 3),
    ):
        qext[base : base + 2, 256 : 256 + Q_LANES] = keep(edge[:, edge_q:EDGE], outside)
        qext[base : base + 2, 0:256] = keep(corner_recv[low_corner, :, 2304:2560], jnp.logical_or(outside, at_left))
        qext[base : base + 2, 256 + Q_LANES : 512 + Q_LANES] = keep(
            corner_recv[high_corner, :, 2304:2560], jnp.logical_or(outside, at_right)
        )
    want = lax.broadcasted_iota(jnp.int32, (64, 48), 0)
    have = lax.broadcasted_iota(jnp.int32, (64, 48), 1)
    slot = want >> 4
    i = want & 15
    source = jnp.where(
        slot == 0,
        jnp.where(i == 0, 33, 2 * i - 1),
        jnp.where(slot == 1, 2 * i, jnp.where(slot == 2, 2 * i + 1, jnp.where(i == 15, 40, 2 * i + 2))),
    )
    pick = jnp.where(source == have, 1.0, 0.0).astype(BF)
    for xe in range(22):
        start = 64 + xe * 192
        low = start // 128 * 128
        picked = jnp.dot(pick, qext[:, low : low + 256], preferred_element_type=F32)
        for t in range(2):
            off = start - low + t * C4
            piece = picked[:, off : off + C4].astype(BF)
            for s in range(4):
                a4[(xe + 1) * 96 + t * 16 : (xe + 1) * 96 + t * 16 + 16, s * 128 : s * 128 + C4] = piece[
                    s * 16 : s * 16 + 16
                ]

    bias4 = widen(b4[...].reshape(1, C4), 128)
    bias4 = jnp.concatenate([bias4, bias4], 1)

    def four(chunk, _):
        parts = []
        for t in range(3):
            for dx in range(3):
                parts.append(
                    jnp.concatenate(
                        [
                            a4[pl.ds(pl.multiple_of((chunk * 5 + x + 1 + dx) * 96 + t * 16, 16), 64), :]
                            for x in range(5)
                        ],
                        0,
                    )
                )
        total = lax.dot_general(
            jnp.concatenate(parts, 1), wt4[...], (((1,), (1,)), ((), ())), preferred_element_type=F32
        )
        total = resid[pl.ds(pl.multiple_of(chunk * 320 + 128, 64), 320), :] + (total + bias4)
        for x in range(5):
            for py in range(2):
                pieces = [
                    total[x * 64 + k * 16 : x * 64 + k * 16 + 16, py * 128 : py * 128 + C4] for k in range(4)
                ]
                line = jnp.concatenate(pieces, 1)
                for tile in range(3):
                    outs[(chunk * 5 + x) * 3 + tile, pl.ds(py, 16, stride=2), :] = line[:, tile * 128 : tile * 128 + 128]
        return 0

    lax.fori_loop(0, 4, four, 0)
    for copy, sends, _gets in copies:

        @pl.when(sends)
        def _(copy=copy):
            copy.wait_send()

    for tile in range(60):
        out[:, tile * 128 : tile * 128 + 128] = outs[tile].astype(BF)


def shards(sizes, section_input, cache_three, gain_three, bias_three, weight_three, weight_up, bias_up, cache_four,
           gain_four, weight_four, bias_four):
    vmem = pl.BlockSpec(memory_space=pltpu.VMEM)
    hbm = pl.BlockSpec(memory_space=pl.ANY)
    scratch = [
        pltpu.VMEM((C3,), F32),
        pltpu.VMEM((C3,), F32),
        pltpu.VMEM((C4,), F32),
        pltpu.VMEM((C4,), F32),
        pltpu.VMEM((C4,), F32),
        pltpu.VMEM((ROWS, X_LANES), BF),
        pltpu.VMEM((ROWS, P_LANES), BF),
        pltpu.VMEM((2 * ROWS, Q_LANES), BF),
        pltpu.VMEM((27, C3 * C3), BF),
        pltpu.VMEM((9, C3 * C4), BF),
        pltpu.VMEM((27, C4 * C4), BF),
        pltpu.VMEM((2, EDGE), BF),
        pltpu.VMEM((2, EDGE), BF),
        pltpu.VMEM((4, 2, CORNER), BF),
        pltpu.VMEM((2, EDGE), BF),
        pltpu.VMEM((2, EDGE), BF),
        pltpu.VMEM((4, 2, CORNER), BF),
        pltpu.VMEM((ROWS, 1536), BF),
        pltpu.VMEM((ROWS, 1536), BF),
        pltpu.VMEM((ROWS, 768), BF),
        pltpu.VMEM((ROWS, 768), BF),
        pltpu.VMEM((2 * ROWS, 256), BF),
        pltpu.VMEM((2 * ROWS, 256), BF),
        pltpu.VMEM((14 * 96, 256), F32),
        pltpu.VMEM((14 * 48, 256), F32),
        pltpu.VMEM((COLS * 64, 256), F32),
        pltpu.VMEM((14 * 144, 768), BF),
        pltpu.VMEM((14 * 96, 768), BF),
        pltpu.VMEM((256, 27 * 256), BF),
        pltpu.VMEM((2, 256, 1536), BF),
        pltpu.VMEM((256, 9 * 512), BF),
        pltpu.VMEM((14 * 96, 768), BF),
        pltpu.VMEM((2, 1152, 256), F32),
        pltpu.VMEM((24 * 96, 512), BF),
        pltpu.VMEM((24 * 64, 256), F32),
        pltpu.VMEM((48, Q_LANES + 512), BF),
        pltpu.VMEM((60, 32, 128), F32),
        pltpu.SemaphoreType.DMA((11,)),
        pltpu.SemaphoreType.DMA((12,)),
        pltpu.SemaphoreType.DMA((12,)),
    ]
    return pl.pallas_call(
        functools.partial(kernel, sizes),
        out_shape=jax.ShapeDtypeStruct((2 * ROWS, 2 * X_LANES // 2), BF),
        in_specs=[hbm] * 11,
        out_specs=vmem,
        scratch_shapes=scratch,
        compiler_params=pltpu.CompilerParams(
            collective_id=0, has_side_effects=True, vmem_limit_bytes=60 * 2**20
        ),
        name="decode",
    )(section_input, cache_three, cache_four, weight_three, weight_up, weight_four, gain_three, bias_three, bias_up,
      gain_four, bias_four)


def solution(mesh):
    sizes = (mesh.shape["row"], mesh.shape["section"], mesh.shape["col"])
    tiled = P("row", ("section", "col"))
    return jax.shard_map(
        functools.partial(shards, sizes),
        mesh=mesh,
        in_specs=(tiled, tiled, P(), P(), P(), P(), P(), tiled, P(), P(), P()),
        out_specs=tiled,
        check_vma=False,
    )
```

```python
import functools

import jax
import jax.numpy as jnp
from jax import lax
from jax.experimental import pallas as pl
from jax.experimental.pallas import tpu as pltpu
from jax.sharding import PartitionSpec as P

EPSILON = 1e-06
MESH = pl.DeviceIdType.MESH
BF = jnp.bfloat16
F32 = jnp.float32
C3 = 192
C4 = 96
ROWS = 16
COLS = 10
FRAMES = 4
BLOCK = 24
X_LANES = COLS * FRAMES * C3
P_LANES = COLS * 2 * C3
Q_LANES = 2 * COLS * 2 * C4
EDGE = X_LANES + P_LANES + Q_LANES
CORNER = 1536 + 768 + 256


def widen(value, lanes):
    pad = lanes - value.shape[1]
    return jnp.concatenate([value, jnp.zeros((value.shape[0], pad), value.dtype)], axis=1)


def norm_act(values, gain, channels):
    meansq = jnp.sum(values * values, axis=-1, keepdims=True) * (1.0 / channels)
    scaled = values * lax.rsqrt(meansq + EPSILON) * gain
    half = 0.5 * scaled
    return half + half * jnp.tanh(half)


def rounded(values):
    return values.astype(BF).astype(F32)


def by_tap(chunk, outs, stride, take):
    taps = chunk.shape[0]
    full = -(-taps // 8) * 8
    wide = jnp.concatenate([chunk, jnp.zeros((full - taps, chunk.shape[1]), chunk.dtype)], 0).astype(F32)
    pieces = []
    for start, count in take:
        stacked = jnp.stack(
            [widen(wide[:, o * stride + start : o * stride + start + count], 128) if count < 128 else
             wide[:, o * stride + start : o * stride + start + count] for o in range(outs)], 0)
        pieces.append(jnp.swapaxes(stacked, 0, 1))
    return pieces


def kernel(
    sizes,
    x_hbm, p_hbm, q_hbm, w3_hbm, wu_hbm, w4_hbm, g3_hbm, b3_hbm, bu_hbm, g4_hbm, b4_hbm,
    out,
    g3, b3, bu, g4, b4,
    xv, pv, qv, w3v, wuv, w4v,
    top, bottom, corner_send,
    from_up, from_down, corner_recv, xl, xr, pl_, pr, ql, qr,
    xs, ps, an, act, act_one, wt3, wtu, wt4, r3s, s4, a4, resid, qext, outs,
    load_sem, send_sem, recv_sem,
):
    row_count, section_count, col_count = sizes
    r = lax.axis_index("row")
    flat_count = section_count * col_count
    g = lax.axis_index("section") * col_count + lax.axis_index("col")
    up, down = lax.rem(r + row_count - 1, row_count), lax.rem(r + 1, row_count)
    left, right = lax.rem(g + flat_count - 1, flat_count), lax.rem(g + 1, flat_count)

    def device(row, flat):
        return {"row": row, "section": flat // col_count, "col": lax.rem(flat, col_count)}

    at_top, at_bottom, at_left, at_right = r == 0, r == row_count - 1, g == 0, g == flat_count - 1
    has_up, has_down, has_left, has_right = r > 0, r < row_count - 1, g > 0, g < flat_count - 1
    up_left, up_right = jnp.logical_and(has_up, has_left), jnp.logical_and(has_up, has_right)
    down_left, down_right = jnp.logical_and(has_down, has_left), jnp.logical_and(has_down, has_right)

    neighbours = [
        (up, left, up_left), (up, g, has_up), (up, right, up_right), (r, left, has_left), (r, right, has_right),
        (down, left, down_left), (down, g, has_down), (down, right, down_right),
    ]
    count_rows = jnp.where(at_top, 0, 1) + jnp.where(at_bottom, 0, 1)
    count_cols = jnp.where(at_left, 0, 1) + jnp.where(at_right, 0, 1)

    loads = [
        pltpu.make_async_copy(src, dst, load_sem.at[i])
        for i, (src, dst) in enumerate(
            ((x_hbm, xv), (p_hbm, pv), (q_hbm, qv), (wu_hbm, wuv), (w4_hbm, w4v), (w3_hbm, w3v),
             (g3_hbm, g3), (b3_hbm, b3), (bu_hbm, bu), (g4_hbm, g4), (b4_hbm, b4))
        )
    ]
    for load in loads[:3]:
        load.start()

    barrier = pltpu.get_barrier_semaphore()
    for row, flat, there in neighbours:

        @pl.when(there)
        def _(row=row, flat=flat):
            pl.semaphore_signal(barrier, inc=1, device_id=device(row, flat), device_id_type=MESH)

    for load in loads[:3]:
        load.wait()
    for buf, rows3, rows4 in ((top, (0, 2), (0, 2)), (bottom, (ROWS - 2, ROWS), (2 * ROWS - 2, 2 * ROWS))):
        buf[:, 0:X_LANES] = xv[rows3[0] : rows3[1], :]
        buf[:, X_LANES : X_LANES + P_LANES] = pv[rows3[0] : rows3[1], :]
        buf[:, X_LANES + P_LANES : EDGE] = qv[rows4[0] : rows4[1], :]
    for index, (rows3, rows4, high) in enumerate(
        (
            ((0, 2), (0, 2), False),
            ((0, 2), (0, 2), True),
            ((ROWS - 2, ROWS), (2 * ROWS - 2, 2 * ROWS), False),
            ((ROWS - 2, ROWS), (2 * ROWS - 2, 2 * ROWS), True),
        )
    ):
        xo, po, qo = (X_LANES - 1536, P_LANES - 768, Q_LANES - 256) if high else (0, 0, 0)
        corner_send[index, :, 0:1536] = xv[rows3[0] : rows3[1], xo : xo + 1536]
        corner_send[index, :, 1536:2304] = pv[rows3[0] : rows3[1], po : po + 768]
        corner_send[index, :, 2304:2560] = qv[rows4[0] : rows4[1], qo : qo + 256]

    for load in loads[3:]:
        load.start()

    pl.semaphore_wait(barrier, (1 + count_rows) * (1 + count_cols) - 1)

    plan = [
        (top, from_down, up, g, has_up, has_down),
        (bottom, from_up, down, g, has_down, has_up),
        (xv.at[:, 0:1536], xr, r, left, has_left, has_right),
        (xv.at[:, X_LANES - 1536 : X_LANES], xl, r, right, has_right, has_left),
        (pv.at[:, 0:768], pr, r, left, has_left, has_right),
        (pv.at[:, P_LANES - 768 : P_LANES], pl_, r, right, has_right, has_left),
        (corner_send.at[0], corner_recv.at[3], up, left, up_left, down_right),
        (corner_send.at[1], corner_recv.at[2], up, right, up_right, down_left),
        (corner_send.at[2], corner_recv.at[1], down, left, down_left, up_right),
        (corner_send.at[3], corner_recv.at[0], down, right, down_right, up_left),
        (qv.at[:, 0:256], qr, r, left, has_left, has_right),
        (qv.at[:, Q_LANES - 256 : Q_LANES], ql, r, right, has_right, has_left),
    ]
    copies = [
        (
            pltpu.make_async_remote_copy(
                src_ref=src,
                dst_ref=dst,
                send_sem=send_sem.at[i],
                recv_sem=recv_sem.at[i],
                device_id=device(row, flat),
                device_id_type=MESH,
            ),
            sends,
            gets,
        )
        for i, (src, dst, row, flat, sends, gets) in enumerate(plan)
    ]
    for copy, sends, _gets in copies:

        @pl.when(sends)
        def _(copy=copy):
            copy.start()

    wt3[...] = jnp.zeros_like(wt3)
    wtu[...] = jnp.zeros_like(wtu)
    wt4[...] = jnp.zeros_like(wt4)
    xs[...] = jnp.zeros_like(xs)
    ps[...] = jnp.zeros_like(ps)
    a4[...] = jnp.zeros_like(a4)
    r3s[0:96, :] = jnp.zeros((96, 768), BF)
    r3s[13 * 96 : 14 * 96, :] = jnp.zeros((96, 768), BF)

    loads[3].wait()

    def up_weights(group, _):
        chunk = wuv[:, pl.ds(pl.multiple_of(group * 16 * C3, 128), 16 * C3)]
        pieces = by_tap(chunk, 16, C3, ((0, 128), (128, 64)))
        for half, taps in enumerate(pieces):
            tap = [[taps[3 * dy + dx] for dx in range(3)] for dy in range(3)]
            across = [
                {(0, 0): line[0], (0, 1): line[1] + line[2], (1, 1): line[0] + line[1], (1, 2): line[2]} for line in tap
            ]
            for (px, dx), _first in across[0].items():
                vals = [line[(px, dx)] for line in across]
                for py, slots in enumerate(((vals[0], vals[1] + vals[2]), (vals[0] + vals[1], vals[2]))):
                    for slot, val in enumerate(slots):
                        lane = dx * 512 + slot * 256 + half * 128
                        wtu[py, pl.ds(pl.multiple_of(px * 128 + group * 16, 16), 16), lane : lane + 128] = val.astype(BF)
        return 0

    lax.fori_loop(0, 6, up_weights, 0)

    loads[4].wait()

    def four_weights(group, _):
        chunk = w4v[:, pl.ds(pl.multiple_of(group * 16 * C4, 128), 16 * C4)]
        (taps,) = by_tap(chunk, 16, C4, ((0, C4),))
        for t in range(3):
            for dx in range(3):
                for dy in range(3):
                    val = taps[9 * t + 3 * dy + dx].astype(BF)
                    for py in range(2):
                        lane = (t * 3 + dx) * 512 + (dy + py) * 128
                        wt4[pl.ds(pl.multiple_of(py * 128 + group * 16, 16), 16), lane : lane + 128] = val
        return 0

    lax.fori_loop(0, 6, four_weights, 0)

    loads[5].wait()

    def three_weights(group, _):
        chunk = w3v[:, pl.ds(pl.multiple_of(group * 16 * C3, 128), 16 * C3)]
        pieces = by_tap(chunk, 16, C3, ((0, 128), (128, 64)))
        for half, taps in enumerate(pieces):
            for t in range(3):
                for dx in range(3):
                    for dy in range(3):
                        lane = ((t * 3 + dx) * 3 + dy) * 256 + half * 128
                        wt3[pl.ds(pl.multiple_of(group * 16, 16), 16), lane : lane + 128] = taps[
                            9 * t + 3 * dy + dx
                        ].astype(BF)
        return 0

    lax.fori_loop(0, 12, three_weights, 0)

    for load in loads[6:]:
        load.wait()

    qext[...] = jnp.zeros_like(qext)
    qext[0:32, 256 : 256 + Q_LANES] = qv[...]
    gain3 = widen(g3[...].reshape(1, C3), 256)
    bias3 = widen(b3[...].reshape(1, C3), 256)

    for je in range(2, 2 + COLS):
        for frames, buf, main in ((FRAMES, xs, xv), (2, ps, pv)):
            wide = frames * C3
            mid = main[:, (je - 2) * wide : (je - 1) * wide].astype(F32)
            for k in range(frames):
                base = (je * frames + k) * BLOCK
                buf[base : base + 16, 0:C3] = mid[:, k * C3 : (k + 1) * C3]

    def own(j, _):
        rows = [xs[pl.ds(pl.multiple_of(j * 96 + 192 + k * BLOCK, 8), 16), :] for k in range(FRAMES)]
        an[pl.ds(pl.multiple_of(j * 64, 64), 64), :] = norm_act(jnp.concatenate(rows, 0), gain3, C3)
        return 0

    lax.fori_loop(0, COLS, own, 0)

    def arrive(group):
        for copy, _sends, gets in group:

            @pl.when(gets)
            def _(copy=copy):
                copy.wait_recv()

    def keep(value, outside):
        return jnp.where(outside, jnp.zeros_like(value), value)

    def edges(je):
        j = je - 2
        for frames, buf, main, low, high, edge_base, corner_base in (
            (FRAMES, xs, xv, xl, xr, 0, 0),
            (2, ps, pv, pl_, pr, X_LANES, 1536),
        ):
            wide = frames * C3
            if j < 0:
                side = at_left
                mid = keep(low[:, je * wide : (je + 1) * wide].astype(F32), side)
                above = corner_recv[0, :, corner_base + je * wide : corner_base + (je + 1) * wide].astype(F32)
                below = corner_recv[2, :, corner_base + je * wide : corner_base + (je + 1) * wide].astype(F32)
            elif j >= COLS:
                side = at_right
                jr = j - COLS
                mid = keep(high[:, jr * wide : (jr + 1) * wide].astype(F32), side)
                above = corner_recv[1, :, corner_base + jr * wide : corner_base + (jr + 1) * wide].astype(F32)
                below = corner_recv[3, :, corner_base + jr * wide : corner_base + (jr + 1) * wide].astype(F32)
            else:
                side = jnp.bool_(False)
                mid = None
                above = from_up[:, edge_base + j * wide : edge_base + (j + 1) * wide].astype(F32)
                below = from_down[:, edge_base + j * wide : edge_base + (j + 1) * wide].astype(F32)
            above = keep(above, jnp.logical_or(side, at_top))
            below = keep(below, jnp.logical_or(side, at_bottom))
            for k in range(frames):
                base = (je * frames + k) * BLOCK
                lanes = slice(k * C3, (k + 1) * C3)
                if mid is not None:
                    buf[base : base + 16, 0:C3] = mid[:, lanes]
                buf[base + 16 : base + 18, 0:C3] = below[:, lanes]
                buf[base + 22 : base + 24, 0:C3] = above[:, lanes]

    def place(je, new):
        old = ps[pl.ds(pl.multiple_of(je * 48, 16), 48), :].reshape(2, BLOCK, 256)
        frames = jnp.concatenate([old, new], 0)
        for slot, shift in enumerate((1, 0, BLOCK - 1)):
            moved = pltpu.roll(frames, shift, axis=1) if shift else frames
            lanes = slice(slot * 256, (slot + 1) * 256)
            act[pl.ds(pl.multiple_of(je * 144, 16), 144), lanes] = moved.reshape(144, 256).astype(BF)
            act_one[pl.ds(pl.multiple_of(je * 96, 32), 96), lanes] = moved[1:5].reshape(96, 256).astype(BF)

    def side_build(i, _):
        je = i + (i // 2) * 10
        raw = xs[pl.ds(pl.multiple_of(je * 96, 32), 96), :]
        place(je, norm_act(raw, gain3, C3).reshape(4, BLOCK, 256))
        return 0

    def own_build(j, _):
        je = j + 2
        rows = [xs[pl.ds(pl.multiple_of(je * 96 + k * BLOCK + 16, 8), 8), :] for k in range(FRAMES)]
        edge = norm_act(jnp.concatenate(rows, 0), gain3, C3).reshape(4, 8, 256)
        main = an[pl.ds(pl.multiple_of(j * 64, 64), 64), :].reshape(4, 16, 256)
        place(je, jnp.concatenate([main, edge], 1))
        return 0

    def three(cols):
        parts = []
        for t in range(3):
            for dx in range(3):
                rows = []
                for c in cols:
                    je = c + dx
                    if t == 1:
                        rows.append(act_one[pl.ds(pl.multiple_of(je * 96, 32), 96), :])
                    else:
                        rows.append(act[pl.ds(pl.multiple_of(je * 144 + 24 * t, 16), 96), :])
                parts.append(jnp.concatenate(rows, 0))
        total = lax.dot_general(
            jnp.concatenate(parts, 1), wt3[...], (((1,), (1,)), ((), ())), preferred_element_type=F32
        )
        rr = lax.broadcasted_iota(jnp.int32, (4, BLOCK, 256), 1)
        up_row = jnp.where(at_top, 23, -1)
        down_row = jnp.where(at_bottom, 16, -1)
        inside_rows = (rr != up_row) & (rr != down_row)
        for n, c in enumerate(cols):
            at = pl.ds(pl.multiple_of(c * 96 + 96, 32), 96)
            piece = xs[at, :] + (total[n * 96 : n * 96 + 96] + bias3)
            outside = jnp.logical_or(jnp.logical_and(at_left, c == 0), jnp.logical_and(at_right, c == 11))
            inside = inside_rows & (rr >= jnp.where(outside, BLOCK, 0))
            piece = rounded(jnp.where(inside, piece.reshape(4, BLOCK, 256), 0.0))
            for slot, shift in enumerate((1, 0, BLOCK - 1)):
                moved = pltpu.roll(piece, shift, axis=1) if shift else piece
                r3s[at, slot * 256 : (slot + 1) * 256] = moved.reshape(96, 256).astype(BF)

    def own_three(i, _):
        three([2 + 4 * i + n for n in range(4)])
        return 0

    bias_u = bu[...].reshape(1, C4)
    bias_u = jnp.concatenate([widen(bias_u, 128)] * 2, 1)

    def upsample(chunk, _):
        for py in range(2):
            parts = [
                r3s[pl.ds(pl.multiple_of(chunk * 384 + dx * 96, 32), 384), py * 256 : py * 256 + 512]
                for dx in range(3)
            ]
            total = lax.dot_general(
                jnp.concatenate(parts, 1), wtu[py], (((1,), (1,)), ((), ())), preferred_element_type=F32
            )
            s4[py, pl.ds(pl.multiple_of(chunk * 384, 128), 384), :] = total + bias_u
        return 0

    gain4 = widen(g4[...].reshape(1, C4), 128)

    def four_in(jj, _):
        for px in range(2):
            acts = []
            at = jj * 2 + px
            for py in range(2):
                value = rounded(s4[py, pl.ds(pl.multiple_of(jj * 96, 32), 96), px * 128 : px * 128 + 128])
                shaped = value.reshape(4, BLOCK, 128)
                resid[pl.ds(pl.multiple_of(at * 64, 64), 64), py * 128 : py * 128 + 128] = shaped[:, 0:16].reshape(64, 128)
                active = norm_act(value, gain4, C4).reshape(4, BLOCK, 128)
                rr = lax.broadcasted_iota(jnp.int32, (4, BLOCK, 128), 1)
                line = jnp.where(at_bottom, 16, -1) if py == 0 else jnp.where(at_top, 23, -1)
                column = jnp.logical_or(jnp.logical_and(at_left, at < 2), jnp.logical_and(at_right, at > 21))
                line = jnp.where(column, -2, line)
                active = jnp.where(jnp.logical_or(rr == line, line == -2), 0.0, active)
                acts.append(active)
            slots = (
                pltpu.roll(acts[1], 1, axis=1),
                acts[0],
                acts[1],
                pltpu.roll(acts[0], BLOCK - 1, axis=1),
            )
            for slot, value in enumerate(slots):
                a4[pl.ds(pl.multiple_of(at * 96 + 32, 32), 64), slot * 128 : slot * 128 + 128] = (
                    value[:, 0:16].reshape(64, 128).astype(BF)
                )
        return 0

    arrive(copies[:2])
    for je in range(2, 2 + COLS):
        edges(je)
    lax.fori_loop(0, COLS, own_build, 0)
    lax.fori_loop(0, 2, own_three, 0)
    upsample(1, 0)
    lax.fori_loop(4, 8, four_in, 0)

    arrive(copies[2:])
    for je in (0, 1, 2 + COLS, 3 + COLS):
        edges(je)
    lax.fori_loop(0, 4, side_build, 0)
    three([0, 1, 10, 11])
    lax.fori_loop(0, 2, lambda i, _: upsample(2 * i, 0), 0)
    lax.fori_loop(0, 8, lambda i, _: four_in(i + i // 4 * 4, 0), 0)

    edge_q = X_LANES + P_LANES
    qext[0:32, 0:256] = keep(ql[...], at_left)
    qext[0:32, 256 + Q_LANES : 512 + Q_LANES] = keep(qr[...], at_right)
    for base, edge, outside, low_corner, high_corner in (
        (32, from_up, at_top, 0, 1),
        (40, from_down, at_bottom, 2, 3),
    ):
        qext[base : base + 2, 256 : 256 + Q_LANES] = keep(edge[:, edge_q:EDGE], outside)
        qext[base : base + 2, 0:256] = keep(corner_recv[low_corner, :, 2304:2560], jnp.logical_or(outside, at_left))
        qext[base : base + 2, 256 + Q_LANES : 512 + Q_LANES] = keep(
            corner_recv[high_corner, :, 2304:2560], jnp.logical_or(outside, at_right)
        )
    want = lax.broadcasted_iota(jnp.int32, (64, 48), 0)
    have = lax.broadcasted_iota(jnp.int32, (64, 48), 1)
    slot = want >> 4
    i = want & 15
    source = jnp.where(
        slot == 0,
        jnp.where(i == 0, 33, 2 * i - 1),
        jnp.where(slot == 1, 2 * i, jnp.where(slot == 2, 2 * i + 1, jnp.where(i == 15, 40, 2 * i + 2))),
    )
    pick = jnp.where(source == have, 1.0, 0.0).astype(BF)
    for xe in range(22):
        start = 64 + xe * 192
        low = start // 128 * 128
        picked = jnp.dot(pick, qext[:, low : low + 256], preferred_element_type=F32)
        for t in range(2):
            off = start - low + t * C4
            piece = picked[:, off : off + C4].astype(BF)
            for s in range(4):
                a4[(xe + 1) * 96 + t * 16 : (xe + 1) * 96 + t * 16 + 16, s * 128 : s * 128 + C4] = piece[
                    s * 16 : s * 16 + 16
                ]

    bias4 = widen(b4[...].reshape(1, C4), 128)
    bias4 = jnp.concatenate([bias4, bias4], 1)

    def four(chunk, _):
        parts = []
        for t in range(3):
            for dx in range(3):
                parts.append(
                    jnp.concatenate(
                        [
                            a4[pl.ds(pl.multiple_of((chunk * 5 + x + 1 + dx) * 96 + t * 16, 16), 64), :]
                            for x in range(5)
                        ],
                        0,
                    )
                )
        total = lax.dot_general(
            jnp.concatenate(parts, 1), wt4[...], (((1,), (1,)), ((), ())), preferred_element_type=F32
        )
        total = resid[pl.ds(pl.multiple_of(chunk * 320 + 128, 64), 320), :] + (total + bias4)
        for x in range(5):
            for py in range(2):
                pieces = [
                    total[x * 64 + k * 16 : x * 64 + k * 16 + 16, py * 128 : py * 128 + C4] for k in range(4)
                ]
                line = jnp.concatenate(pieces, 1)
                for tile in range(3):
                    outs[(chunk * 5 + x) * 3 + tile, pl.ds(py, 16, stride=2), :] = line[:, tile * 128 : tile * 128 + 128]
        return 0

    lax.fori_loop(0, 4, four, 0)
    for copy, sends, _gets in copies:

        @pl.when(sends)
        def _(copy=copy):
            copy.wait_send()

    for tile in range(60):
        out[:, tile * 128 : tile * 128 + 128] = outs[tile].astype(BF)


def shards(sizes, section_input, cache_three, gain_three, bias_three, weight_three, weight_up, bias_up, cache_four,
           gain_four, weight_four, bias_four):
    vmem = pl.BlockSpec(memory_space=pltpu.VMEM)
    hbm = pl.BlockSpec(memory_space=pl.ANY)
    scratch = [
        pltpu.VMEM((C3,), F32),
        pltpu.VMEM((C3,), F32),
        pltpu.VMEM((C4,), F32),
        pltpu.VMEM((C4,), F32),
        pltpu.VMEM((C4,), F32),
        pltpu.VMEM((ROWS, X_LANES), BF),
        pltpu.VMEM((ROWS, P_LANES), BF),
        pltpu.VMEM((2 * ROWS, Q_LANES), BF),
        pltpu.VMEM((27, C3 * C3), BF),
        pltpu.VMEM((9, C3 * C4), BF),
        pltpu.VMEM((27, C4 * C4), BF),
        pltpu.VMEM((2, EDGE), BF),
        pltpu.VMEM((2, EDGE), BF),
        pltpu.VMEM((4, 2, CORNER), BF),
        pltpu.VMEM((2, EDGE), BF),
        pltpu.VMEM((2, EDGE), BF),
        pltpu.VMEM((4, 2, CORNER), BF),
        pltpu.VMEM((ROWS, 1536), BF),
        pltpu.VMEM((ROWS, 1536), BF),
        pltpu.VMEM((ROWS, 768), BF),
        pltpu.VMEM((ROWS, 768), BF),
        pltpu.VMEM((2 * ROWS, 256), BF),
        pltpu.VMEM((2 * ROWS, 256), BF),
        pltpu.VMEM((14 * 96, 256), F32),
        pltpu.VMEM((14 * 48, 256), F32),
        pltpu.VMEM((COLS * 64, 256), F32),
        pltpu.VMEM((14 * 144, 768), BF),
        pltpu.VMEM((14 * 96, 768), BF),
        pltpu.VMEM((256, 27 * 256), BF),
        pltpu.VMEM((2, 256, 1536), BF),
        pltpu.VMEM((256, 9 * 512), BF),
        pltpu.VMEM((14 * 96, 768), BF),
        pltpu.VMEM((2, 1152, 256), F32),
        pltpu.VMEM((24 * 96, 512), BF),
        pltpu.VMEM((24 * 64, 256), F32),
        pltpu.VMEM((48, Q_LANES + 512), BF),
        pltpu.VMEM((60, 32, 128), F32),
        pltpu.SemaphoreType.DMA((11,)),
        pltpu.SemaphoreType.DMA((12,)),
        pltpu.SemaphoreType.DMA((12,)),
    ]
    return pl.pallas_call(
        functools.partial(kernel, sizes),
        out_shape=jax.ShapeDtypeStruct((2 * ROWS, 2 * X_LANES // 2), BF),
        in_specs=[hbm] * 11,
        out_specs=vmem,
        scratch_shapes=scratch,
        compiler_params=pltpu.CompilerParams(
            collective_id=0, has_side_effects=True, vmem_limit_bytes=60 * 2**20
        ),
        name="decode",
    )(section_input, cache_three, cache_four, weight_three, weight_up, weight_four, gain_three, bias_three, bias_up,
      gain_four, bias_four)


def solution(mesh):
    sizes = (mesh.shape["row"], mesh.shape["section"], mesh.shape["col"])
    tiled = P("row", ("section", "col"))
    return jax.shard_map(
        functools.partial(shards, sizes),
        mesh=mesh,
        in_specs=(tiled, tiled, P(), P(), P(), P(), P(), tiled, P(), P(), P()),
        out_specs=tiled,
        check_vma=False,
    )
```

```python
import functools

import jax
import jax.numpy as jnp
from jax import lax
from jax.experimental import pallas as pl
from jax.experimental.pallas import tpu as pltpu
from jax.sharding import PartitionSpec as P

EPSILON = 1e-06
MESH = pl.DeviceIdType.MESH
BF = jnp.bfloat16
F32 = jnp.float32
C3 = 192
C4 = 96
ROWS = 16
COLS = 10
FRAMES = 4
BLOCK = 24
X_LANES = COLS * FRAMES * C3
P_LANES = COLS * 2 * C3
Q_LANES = 2 * COLS * 2 * C4
EDGE = X_LANES + P_LANES + Q_LANES
CORNER = 1536 + 768 + 256


def widen(value, lanes):
    pad = lanes - value.shape[1]
    return jnp.concatenate([value, jnp.zeros((value.shape[0], pad), value.dtype)], axis=1)


def norm_act(values, gain, channels):
    meansq = jnp.sum(values * values, axis=-1, keepdims=True) * (1.0 / channels)
    scaled = values * lax.rsqrt(meansq + EPSILON) * gain
    half = 0.5 * scaled
    return half + half * jnp.tanh(half)


def rounded(values):
    return values.astype(BF).astype(F32)


def by_tap(chunk, outs, stride, take):
    taps = chunk.shape[0]
    full = -(-taps // 8) * 8
    wide = jnp.concatenate([chunk, jnp.zeros((full - taps, chunk.shape[1]), chunk.dtype)], 0).astype(F32)
    pieces = []
    for start, count in take:
        stacked = jnp.stack(
            [widen(wide[:, o * stride + start : o * stride + start + count], 128) if count < 128 else
             wide[:, o * stride + start : o * stride + start + count] for o in range(outs)], 0)
        pieces.append(jnp.swapaxes(stacked, 0, 1))
    return pieces


def kernel(
    sizes,
    x_hbm, p_hbm, q_hbm, w3_hbm, wu_hbm, w4_hbm, g3_hbm, b3_hbm, bu_hbm, g4_hbm, b4_hbm,
    out,
    g3, b3, bu, g4, b4,
    xv, pv, qv, w3v, wuv, w4v,
    top, bottom, corner_send,
    from_up, from_down, corner_recv, xl, xr, pl_, pr, ql, qr,
    xs, ps, an, act, act_one, wt3, wtu, wt4, r3s, s4, a4, resid, qext, outs,
    load_sem, send_sem, recv_sem,
):
    row_count, section_count, col_count = sizes
    r = lax.axis_index("row")
    flat_count = section_count * col_count
    g = lax.axis_index("section") * col_count + lax.axis_index("col")
    up, down = lax.rem(r + row_count - 1, row_count), lax.rem(r + 1, row_count)
    left, right = lax.rem(g + flat_count - 1, flat_count), lax.rem(g + 1, flat_count)

    def device(row, flat):
        return {"row": row, "section": flat // col_count, "col": lax.rem(flat, col_count)}

    at_top, at_bottom, at_left, at_right = r == 0, r == row_count - 1, g == 0, g == flat_count - 1
    has_up, has_down, has_left, has_right = r > 0, r < row_count - 1, g > 0, g < flat_count - 1
    up_left, up_right = jnp.logical_and(has_up, has_left), jnp.logical_and(has_up, has_right)
    down_left, down_right = jnp.logical_and(has_down, has_left), jnp.logical_and(has_down, has_right)

    neighbours = [
        (up, left, up_left), (up, g, has_up), (up, right, up_right), (r, left, has_left), (r, right, has_right),
        (down, left, down_left), (down, g, has_down), (down, right, down_right),
    ]
    count_rows = jnp.where(at_top, 0, 1) + jnp.where(at_bottom, 0, 1)
    count_cols = jnp.where(at_left, 0, 1) + jnp.where(at_right, 0, 1)

    loads = [
        pltpu.make_async_copy(src, dst, load_sem.at[i])
        for i, (src, dst) in enumerate(
            ((x_hbm, xv), (p_hbm, pv), (q_hbm, qv), (wu_hbm, wuv), (w4_hbm, w4v), (w3_hbm, w3v),
             (g3_hbm, g3), (b3_hbm, b3), (bu_hbm, bu), (g4_hbm, g4), (b4_hbm, b4))
        )
    ]
    for load in loads[:3]:
        load.start()

    barrier = pltpu.get_barrier_semaphore()
    for row, flat, there in neighbours:

        @pl.when(there)
        def _(row=row, flat=flat):
            pl.semaphore_signal(barrier, inc=1, device_id=device(row, flat), device_id_type=MESH)

    for load in loads[:3]:
        load.wait()
    for buf, rows3, rows4 in ((top, (0, 2), (0, 2)), (bottom, (ROWS - 2, ROWS), (2 * ROWS - 2, 2 * ROWS))):
        buf[:, 0:X_LANES] = xv[rows3[0] : rows3[1], :]
        buf[:, X_LANES : X_LANES + P_LANES] = pv[rows3[0] : rows3[1], :]
        buf[:, X_LANES + P_LANES : EDGE] = qv[rows4[0] : rows4[1], :]
    for index, (rows3, rows4, high) in enumerate(
        (
            ((0, 2), (0, 2), False),
            ((0, 2), (0, 2), True),
            ((ROWS - 2, ROWS), (2 * ROWS - 2, 2 * ROWS), False),
            ((ROWS - 2, ROWS), (2 * ROWS - 2, 2 * ROWS), True),
        )
    ):
        xo, po, qo = (X_LANES - 1536, P_LANES - 768, Q_LANES - 256) if high else (0, 0, 0)
        corner_send[index, :, 0:1536] = xv[rows3[0] : rows3[1], xo : xo + 1536]
        corner_send[index, :, 1536:2304] = pv[rows3[0] : rows3[1], po : po + 768]
        corner_send[index, :, 2304:2560] = qv[rows4[0] : rows4[1], qo : qo + 256]

    for load in loads[3:]:
        load.start()

    pl.semaphore_wait(barrier, (1 + count_rows) * (1 + count_cols) - 1)

    plan = [
        (top, from_down, up, g, has_up, has_down),
        (bottom, from_up, down, g, has_down, has_up),
        (xv.at[:, 0:1536], xr, r, left, has_left, has_right),
        (xv.at[:, X_LANES - 1536 : X_LANES], xl, r, right, has_right, has_left),
        (pv.at[:, 0:768], pr, r, left, has_left, has_right),
        (pv.at[:, P_LANES - 768 : P_LANES], pl_, r, right, has_right, has_left),
        (corner_send.at[0], corner_recv.at[3], up, left, up_left, down_right),
        (corner_send.at[1], corner_recv.at[2], up, right, up_right, down_left),
        (corner_send.at[2], corner_recv.at[1], down, left, down_left, up_right),
        (corner_send.at[3], corner_recv.at[0], down, right, down_right, up_left),
        (qv.at[:, 0:256], qr, r, left, has_left, has_right),
        (qv.at[:, Q_LANES - 256 : Q_LANES], ql, r, right, has_right, has_left),
    ]
    copies = [
        (
            pltpu.make_async_remote_copy(
                src_ref=src,
                dst_ref=dst,
                send_sem=send_sem.at[i],
                recv_sem=recv_sem.at[i],
                device_id=device(row, flat),
                device_id_type=MESH,
            ),
            sends,
            gets,
        )
        for i, (src, dst, row, flat, sends, gets) in enumerate(plan)
    ]
    for copy, sends, _gets in copies:

        @pl.when(sends)
        def _(copy=copy):
            copy.start()

    wt3[...] = jnp.zeros_like(wt3)
    wtu[...] = jnp.zeros_like(wtu)
    wt4[...] = jnp.zeros_like(wt4)
    xs[...] = jnp.zeros_like(xs)
    ps[...] = jnp.zeros_like(ps)
    a4[...] = jnp.zeros_like(a4)
    r3s[0:96, :] = jnp.zeros((96, 768), BF)
    r3s[13 * 96 : 14 * 96, :] = jnp.zeros((96, 768), BF)

    loads[3].wait()

    def up_weights(group, _):
        chunk = wuv[:, pl.ds(pl.multiple_of(group * 16 * C3, 128), 16 * C3)]
        pieces = by_tap(chunk, 16, C3, ((0, 128), (128, 64)))
        for half, taps in enumerate(pieces):
            tap = [[taps[3 * dy + dx] for dx in range(3)] for dy in range(3)]
            across = [
                {(0, 0): line[0], (0, 1): line[1] + line[2], (1, 1): line[0] + line[1], (1, 2): line[2]} for line in tap
            ]
            for (px, dx), _first in across[0].items():
                vals = [line[(px, dx)] for line in across]
                for py, slots in enumerate(((vals[0], vals[1] + vals[2]), (vals[0] + vals[1], vals[2]))):
                    for slot, val in enumerate(slots):
                        lane = dx * 512 + slot * 256 + half * 128
                        wtu[py, pl.ds(pl.multiple_of(px * 128 + group * 16, 16), 16), lane : lane + 128] = val.astype(BF)
        return 0

    lax.fori_loop(0, 6, up_weights, 0)

    loads[4].wait()

    def four_weights(group, _):
        chunk = w4v[:, pl.ds(pl.multiple_of(group * 16 * C4, 128), 16 * C4)]
        (taps,) = by_tap(chunk, 16, C4, ((0, C4),))
        for t in range(3):
            for dx in range(3):
                for dy in range(3):
                    val = taps[9 * t + 3 * dy + dx].astype(BF)
                    for py in range(2):
                        lane = (t * 3 + dx) * 512 + (dy + py) * 128
                        wt4[pl.ds(pl.multiple_of(py * 128 + group * 16, 16), 16), lane : lane + 128] = val
        return 0

    lax.fori_loop(0, 6, four_weights, 0)

    loads[5].wait()

    def three_weights(group, _):
        chunk = w3v[:, pl.ds(pl.multiple_of(group * 16 * C3, 128), 16 * C3)]
        pieces = by_tap(chunk, 16, C3, ((0, 128), (128, 64)))
        for half, taps in enumerate(pieces):
            for t in range(3):
                for dx in range(3):
                    for dy in range(3):
                        lane = ((t * 3 + dx) * 3 + dy) * 256 + half * 128
                        wt3[pl.ds(pl.multiple_of(group * 16, 16), 16), lane : lane + 128] = taps[
                            9 * t + 3 * dy + dx
                        ].astype(BF)
        return 0

    lax.fori_loop(0, 12, three_weights, 0)

    for load in loads[6:]:
        load.wait()

    qext[...] = jnp.zeros_like(qext)
    qext[0:32, 256 : 256 + Q_LANES] = qv[...]
    gain3 = widen(g3[...].reshape(1, C3), 256)
    bias3 = widen(b3[...].reshape(1, C3), 256)

    for je in range(2, 2 + COLS):
        for frames, buf, main in ((FRAMES, xs, xv), (2, ps, pv)):
            wide = frames * C3
            mid = main[:, (je - 2) * wide : (je - 1) * wide].astype(F32)
            for k in range(frames):
                base = (je * frames + k) * BLOCK
                buf[base : base + 16, 0:C3] = mid[:, k * C3 : (k + 1) * C3]

    def own(j, _):
        rows = [xs[pl.ds(pl.multiple_of(j * 96 + 192 + k * BLOCK, 8), 16), :] for k in range(FRAMES)]
        an[pl.ds(pl.multiple_of(j * 64, 64), 64), :] = norm_act(jnp.concatenate(rows, 0), gain3, C3)
        return 0

    lax.fori_loop(0, COLS, own, 0)

    for copy, sends, gets in copies:

        @pl.when(gets)
        def _(copy=copy):
            copy.wait_recv()

    def keep(value, outside):
        return jnp.where(outside, jnp.zeros_like(value), value)

    for je in range(14):
        j = je - 2
        for frames, buf, main, low, high, edge_base, corner_base in (
            (FRAMES, xs, xv, xl, xr, 0, 0),
            (2, ps, pv, pl_, pr, X_LANES, 1536),
        ):
            wide = frames * C3
            if j < 0:
                side = at_left
                mid = keep(low[:, je * wide : (je + 1) * wide].astype(F32), side)
                above = corner_recv[0, :, corner_base + je * wide : corner_base + (je + 1) * wide].astype(F32)
                below = corner_recv[2, :, corner_base + je * wide : corner_base + (je + 1) * wide].astype(F32)
            elif j >= COLS:
                side = at_right
                jr = j - COLS
                mid = keep(high[:, jr * wide : (jr + 1) * wide].astype(F32), side)
                above = corner_recv[1, :, corner_base + jr * wide : corner_base + (jr + 1) * wide].astype(F32)
                below = corner_recv[3, :, corner_base + jr * wide : corner_base + (jr + 1) * wide].astype(F32)
            else:
                side = jnp.bool_(False)
                mid = None
                above = from_up[:, edge_base + j * wide : edge_base + (j + 1) * wide].astype(F32)
                below = from_down[:, edge_base + j * wide : edge_base + (j + 1) * wide].astype(F32)
            above = keep(above, jnp.logical_or(side, at_top))
            below = keep(below, jnp.logical_or(side, at_bottom))
            for k in range(frames):
                base = (je * frames + k) * BLOCK
                lanes = slice(k * C3, (k + 1) * C3)
                if mid is not None:
                    buf[base : base + 16, 0:C3] = mid[:, lanes]
                buf[base + 16 : base + 18, 0:C3] = below[:, lanes]
                buf[base + 22 : base + 24, 0:C3] = above[:, lanes]

    def place(je, new):
        old = ps[pl.ds(pl.multiple_of(je * 48, 16), 48), :].reshape(2, BLOCK, 256)
        frames = jnp.concatenate([old, new], 0)
        for slot, shift in enumerate((1, 0, BLOCK - 1)):
            moved = pltpu.roll(frames, shift, axis=1) if shift else frames
            lanes = slice(slot * 256, (slot + 1) * 256)
            act[pl.ds(pl.multiple_of(je * 144, 16), 144), lanes] = moved.reshape(144, 256).astype(BF)
            act_one[pl.ds(pl.multiple_of(je * 96, 32), 96), lanes] = moved[1:5].reshape(96, 256).astype(BF)

    def side_build(i, _):
        je = i + (i // 2) * 10
        raw = xs[pl.ds(pl.multiple_of(je * 96, 32), 96), :]
        place(je, norm_act(raw, gain3, C3).reshape(4, BLOCK, 256))
        return 0

    def own_build(j, _):
        je = j + 2
        rows = [xs[pl.ds(pl.multiple_of(je * 96 + k * BLOCK + 16, 8), 8), :] for k in range(FRAMES)]
        edge = norm_act(jnp.concatenate(rows, 0), gain3, C3).reshape(4, 8, 256)
        main = an[pl.ds(pl.multiple_of(j * 64, 64), 64), :].reshape(4, 16, 256)
        place(je, jnp.concatenate([main, edge], 1))
        return 0

    lax.fori_loop(0, 4, side_build, 0, unroll=4)
    lax.fori_loop(0, COLS, own_build, 0, unroll=5)

    def three(chunk, _):
        parts = []
        for t in range(3):
            for dx in range(3):
                rows = []
                for j in range(4):
                    je = chunk * 4 + j + dx
                    if t == 1:
                        rows.append(act_one[pl.ds(pl.multiple_of(je * 96, 32), 96), :])
                    else:
                        rows.append(act[pl.ds(pl.multiple_of(je * 144 + 24 * t, 16), 96), :])
                parts.append(jnp.concatenate(rows, 0))
        total = lax.dot_general(
            jnp.concatenate(parts, 1), wt3[...], (((1,), (1,)), ((), ())), preferred_element_type=F32
        )
        total = xs[pl.ds(pl.multiple_of(chunk * 384 + 96, 32), 384), :] + (total + bias3)
        total = total.reshape(16, BLOCK, 256)
        blk = lax.broadcasted_iota(jnp.int32, (16, BLOCK, 256), 0) + chunk * 16
        rr = lax.broadcasted_iota(jnp.int32, (16, BLOCK, 256), 1)
        lowest = jnp.where(at_left, 4, 0)
        highest = jnp.where(at_right, 44, 48)
        up_row = jnp.where(at_top, 23, -1)
        down_row = jnp.where(at_bottom, 16, -1)
        inside = (blk >= lowest) & (blk < highest) & (rr != up_row) & (rr != down_row)
        total = rounded(jnp.where(inside, total, 0.0))
        for slot, shift in enumerate((1, 0, BLOCK - 1)):
            moved = pltpu.roll(total, shift, axis=1) if shift else total
            r3s[pl.ds(pl.multiple_of(chunk * 384 + 96, 32), 384), slot * 256 : (slot + 1) * 256] = moved.reshape(
                384, 256
            ).astype(BF)
        return 0

    lax.fori_loop(0, 3, three, 0, unroll=3)

    bias_u = bu[...].reshape(1, C4)
    bias_u = jnp.concatenate([widen(bias_u, 128)] * 2, 1)

    def upsample(chunk, _):
        for py in range(2):
            parts = [
                r3s[pl.ds(pl.multiple_of(chunk * 384 + dx * 96, 32), 384), py * 256 : py * 256 + 512]
                for dx in range(3)
            ]
            total = lax.dot_general(
                jnp.concatenate(parts, 1), wtu[py], (((1,), (1,)), ((), ())), preferred_element_type=F32
            )
            s4[py, pl.ds(pl.multiple_of(chunk * 384, 128), 384), :] = total + bias_u
        return 0

    lax.fori_loop(0, 3, upsample, 0, unroll=3)

    gain4 = widen(g4[...].reshape(1, C4), 128)

    def four_in(jj, _):
        for px in range(2):
            acts = []
            at = jj * 2 + px
            for py in range(2):
                value = rounded(s4[py, pl.ds(pl.multiple_of(jj * 96, 32), 96), px * 128 : px * 128 + 128])
                shaped = value.reshape(4, BLOCK, 128)
                resid[pl.ds(pl.multiple_of(at * 64, 64), 64), py * 128 : py * 128 + 128] = shaped[:, 0:16].reshape(64, 128)
                active = norm_act(value, gain4, C4).reshape(4, BLOCK, 128)
                rr = lax.broadcasted_iota(jnp.int32, (4, BLOCK, 128), 1)
                line = jnp.where(at_bottom, 16, -1) if py == 0 else jnp.where(at_top, 23, -1)
                column = jnp.logical_or(jnp.logical_and(at_left, at < 2), jnp.logical_and(at_right, at > 21))
                line = jnp.where(column, -2, line)
                active = jnp.where(jnp.logical_or(rr == line, line == -2), 0.0, active)
                acts.append(active)
            slots = (
                pltpu.roll(acts[1], 1, axis=1),
                acts[0],
                acts[1],
                pltpu.roll(acts[0], BLOCK - 1, axis=1),
            )
            for slot, value in enumerate(slots):
                a4[pl.ds(pl.multiple_of(at * 96 + 32, 32), 64), slot * 128 : slot * 128 + 128] = (
                    value[:, 0:16].reshape(64, 128).astype(BF)
                )
        return 0

    lax.fori_loop(0, 12, four_in, 0, unroll=4)

    edge_q = X_LANES + P_LANES
    qext[0:32, 0:256] = keep(ql[...], at_left)
    qext[0:32, 256 + Q_LANES : 512 + Q_LANES] = keep(qr[...], at_right)
    for base, edge, outside, low_corner, high_corner in (
        (32, from_up, at_top, 0, 1),
        (40, from_down, at_bottom, 2, 3),
    ):
        qext[base : base + 2, 256 : 256 + Q_LANES] = keep(edge[:, edge_q:EDGE], outside)
        qext[base : base + 2, 0:256] = keep(corner_recv[low_corner, :, 2304:2560], jnp.logical_or(outside, at_left))
        qext[base : base + 2, 256 + Q_LANES : 512 + Q_LANES] = keep(
            corner_recv[high_corner, :, 2304:2560], jnp.logical_or(outside, at_right)
        )
    want = lax.broadcasted_iota(jnp.int32, (64, 48), 0)
    have = lax.broadcasted_iota(jnp.int32, (64, 48), 1)
    slot = want >> 4
    i = want & 15
    source = jnp.where(
        slot == 0,
        jnp.where(i == 0, 33, 2 * i - 1),
        jnp.where(slot == 1, 2 * i, jnp.where(slot == 2, 2 * i + 1, jnp.where(i == 15, 40, 2 * i + 2))),
    )
    pick = jnp.where(source == have, 1.0, 0.0).astype(BF)
    for xe in range(22):
        start = 64 + xe * 192
        low = start // 128 * 128
        picked = jnp.dot(pick, qext[:, low : low + 256], preferred_element_type=F32)
        for t in range(2):
            off = start - low + t * C4
            piece = picked[:, off : off + C4].astype(BF)
            for s in range(4):
                a4[(xe + 1) * 96 + t * 16 : (xe + 1) * 96 + t * 16 + 16, s * 128 : s * 128 + C4] = piece[
                    s * 16 : s * 16 + 16
                ]

    bias4 = widen(b4[...].reshape(1, C4), 128)
    bias4 = jnp.concatenate([bias4, bias4], 1)

    def four(chunk, _):
        parts = []
        for t in range(3):
            for dx in range(3):
                parts.append(
                    jnp.concatenate(
                        [
                            a4[pl.ds(pl.multiple_of((chunk * 5 + x + 1 + dx) * 96 + t * 16, 16), 64), :]
                            for x in range(5)
                        ],
                        0,
                    )
                )
        total = lax.dot_general(
            jnp.concatenate(parts, 1), wt4[...], (((1,), (1,)), ((), ())), preferred_element_type=F32
        )
        total = resid[pl.ds(pl.multiple_of(chunk * 320 + 128, 64), 320), :] + (total + bias4)
        for x in range(5):
            for py in range(2):
                pieces = [
                    total[x * 64 + k * 16 : x * 64 + k * 16 + 16, py * 128 : py * 128 + C4] for k in range(4)
                ]
                line = jnp.concatenate(pieces, 1)
                for tile in range(3):
                    outs[(chunk * 5 + x) * 3 + tile, pl.ds(py, 16, stride=2), :] = line[:, tile * 128 : tile * 128 + 128]
        return 0

    lax.fori_loop(0, 4, four, 0, unroll=2)
    for copy, sends, _gets in copies:

        @pl.when(sends)
        def _(copy=copy):
            copy.wait_send()

    for tile in range(60):
        out[:, tile * 128 : tile * 128 + 128] = outs[tile].astype(BF)


def shards(sizes, section_input, cache_three, gain_three, bias_three, weight_three, weight_up, bias_up, cache_four,
           gain_four, weight_four, bias_four):
    vmem = pl.BlockSpec(memory_space=pltpu.VMEM)
    hbm = pl.BlockSpec(memory_space=pl.ANY)
    scratch = [
        pltpu.VMEM((C3,), F32),
        pltpu.VMEM((C3,), F32),
        pltpu.VMEM((C4,), F32),
        pltpu.VMEM((C4,), F32),
        pltpu.VMEM((C4,), F32),
        pltpu.VMEM((ROWS, X_LANES), BF),
        pltpu.VMEM((ROWS, P_LANES), BF),
        pltpu.VMEM((2 * ROWS, Q_LANES), BF),
        pltpu.VMEM((27, C3 * C3), BF),
        pltpu.VMEM((9, C3 * C4), BF),
        pltpu.VMEM((27, C4 * C4), BF),
        pltpu.VMEM((2, EDGE), BF),
        pltpu.VMEM((2, EDGE), BF),
        pltpu.VMEM((4, 2, CORNER), BF),
        pltpu.VMEM((2, EDGE), BF),
        pltpu.VMEM((2, EDGE), BF),
        pltpu.VMEM((4, 2, CORNER), BF),
        pltpu.VMEM((ROWS, 1536), BF),
        pltpu.VMEM((ROWS, 1536), BF),
        pltpu.VMEM((ROWS, 768), BF),
        pltpu.VMEM((ROWS, 768), BF),
        pltpu.VMEM((2 * ROWS, 256), BF),
        pltpu.VMEM((2 * ROWS, 256), BF),
        pltpu.VMEM((14 * 96, 256), F32),
        pltpu.VMEM((14 * 48, 256), F32),
        pltpu.VMEM((COLS * 64, 256), F32),
        pltpu.VMEM((14 * 144, 768), BF),
        pltpu.VMEM((14 * 96, 768), BF),
        pltpu.VMEM((256, 27 * 256), BF),
        pltpu.VMEM((2, 256, 1536), BF),
        pltpu.VMEM((256, 9 * 512), BF),
        pltpu.VMEM((14 * 96, 768), BF),
        pltpu.VMEM((2, 1152, 256), F32),
        pltpu.VMEM((24 * 96, 512), BF),
        pltpu.VMEM((24 * 64, 256), F32),
        pltpu.VMEM((48, Q_LANES + 512), BF),
        pltpu.VMEM((60, 32, 128), F32),
        pltpu.SemaphoreType.DMA((11,)),
        pltpu.SemaphoreType.DMA((12,)),
        pltpu.SemaphoreType.DMA((12,)),
    ]
    return pl.pallas_call(
        functools.partial(kernel, sizes),
        out_shape=jax.ShapeDtypeStruct((2 * ROWS, 2 * X_LANES // 2), BF),
        in_specs=[hbm] * 11,
        out_specs=vmem,
        scratch_shapes=scratch,
        compiler_params=pltpu.CompilerParams(
            collective_id=0, has_side_effects=True, vmem_limit_bytes=60 * 2**20
        ),
        name="decode",
    )(section_input, cache_three, cache_four, weight_three, weight_up, weight_four, gain_three, bias_three, bias_up,
      gain_four, bias_four)


def solution(mesh):
    sizes = (mesh.shape["row"], mesh.shape["section"], mesh.shape["col"])
    tiled = P("row", ("section", "col"))
    return jax.shard_map(
        functools.partial(shards, sizes),
        mesh=mesh,
        in_specs=(tiled, tiled, P(), P(), P(), P(), P(), tiled, P(), P(), P()),
        out_specs=tiled,
        check_vma=False,
    )
```
